32 devices in a mesh: dp: 4 (over x, core), fsdp: 8 (over z, y).
Axes of the slice: x: 2, y: 2, z: 4, core: 2. Of those that a mesh axis runs over, the one named last changes fastest.
Arguments:
- inputs: bfloat16 [32768, 1024], P(('dp', 'fsdp')), may hold values from -6 to 6
- lengths: int32 [32], P(('dp', 'fsdp')), may hold values from 256 to 1024, as said below
- query_weight: bfloat16 [1024, 1024], P(None, ('dp', 'fsdp')), may hold values from -0.1875 to 0.1875
- key_weight: bfloat16 [1024, 1024], P(None, ('dp', 'fsdp')), may hold values from -0.1875 to 0.1875
- value_weight: bfloat16 [1024, 1024], P(None, ('dp', 'fsdp')), may hold values from -0.1875 to 0.1875
- gate_weight: bfloat16 [1024, 1024], P(None, ('dp', 'fsdp')), may hold values from -0.1875 to 0.1875
- out_weight: bfloat16 [1024, 1024], P(None, ('dp', 'fsdp')), may hold values from -0.1875 to 0.1875
- first_weight: bfloat16 [1024, 2816], P(None, ('dp', 'fsdp')), may hold values from -0.1875 to 0.1875
- second_weight: bfloat16 [1024, 2816], P(None, ('dp', 'fsdp')), may hold values from -0.1875 to 0.1875
- down_weight: bfloat16 [2816, 1024], P(None, ('dp', 'fsdp')), may hold values from -0.109375 to 0.109375
- cotangent: bfloat16 [32768, 1024], P(('dp', 'fsdp')), may hold values from -6 to 6
Outputs:
- outputs: bfloat16 [32768, 1024], P(('dp', 'fsdp'))
- input_grad: float32 [32768, 1024], P(('dp', 'fsdp'))
- query_grad: float32 [1024, 1024], P(None, ('dp', 'fsdp'))
- key_grad: float32 [1024, 1024], P(None, ('dp', 'fsdp'))
- value_grad: float32 [1024, 1024], P(None, ('dp', 'fsdp'))
- gate_grad: float32 [1024, 1024], P(None, ('dp', 'fsdp'))
- out_grad: float32 [1024, 1024], P(None, ('dp', 'fsdp'))
- first_grad: float32 [1024, 2816], P(None, ('dp', 'fsdp'))
- second_grad: float32 [1024, 2816], P(None, ('dp', 'fsdp'))
- down_grad: float32 [2816, 1024], P(None, ('dp', 'fsdp'))
The draws below stay inside these ranges and needn't reach their ends.
Inputs may be any that keep to these rules, and one draw needn't show every extreme that they name: `lengths`: one length for each sequence; at least one sequence fills all 1024 slots.
All inputs are finite; a program needn't handle non-finite values.
Results may differ from the reference program's by a relative error of at most 0.014.
Values may be sent and summed in bfloat16 or wider, within the bound.
No kernel may reach another device: no remote copies, remote signals or barrier semaphores. Data moves between devices by JAX's collectives and lax.ppermute only.
A program may use at most 320 MiB of HBM per device.

```python
import math
import jax
import jax.numpy as jnp
from jax import lax

D = 1024
HEADS = 8
HEAD = 128
FF = 2816
SPAN = 256
LAYER = 12
LAYERS = 24
SHORTEST = 256
TOK_DEV = 1024
SEQS = 32
TOKENS = 32768


def draw_lengths(key, part):
    extent = TOK_DEV - SHORTEST
    first_key = jax.random.fold_in(key, 11)
    second_key = jax.random.fold_in(key, 12)
    drawn = jax.random.randint(first_key, (SEQS,), 0, extent + 1)
    counts = SHORTEST + drawn * drawn // extent
    chosen = jax.random.randint(second_key, (), 0, SEQS)
    counts = jnp.where(jnp.arange(SEQS) == chosen, TOK_DEV, counts)
    return counts.astype(jnp.int32)


def with_spikes(values, own_key, source, target, parts, factor):
    def block_of(position):
        return (jnp.arange(values.shape[position]) // (values.shape[position] // parts)).reshape((-1,) + (1,) * (values.ndim - 1 - position))

    near = jax.random.permutation(own_key, parts)[block_of(target)]
    far = (block_of(target) + parts // 2) % parts
    return jnp.where((block_of(source) == near) | (block_of(source) == far), factor * values, values)


def levels(key, shape, split, low, high):
    level, own = 1.0, jax.random.fold_in(key, 6)
    for position, parts in split:
        draws = jnp.exp(jax.random.uniform(jax.random.fold_in(own, position), (parts,), jnp.float32, low / len(split), high / len(split)))
        level = level * jnp.repeat(draws, shape[position] // parts).reshape([-1 if axis == position else 1 for axis in range(len(shape))])
    return level


def scatter_about(own_key, dims, width, bound, cuts=(), held_as=jnp.bfloat16):
    array = jax.random.normal(own_key, dims, jnp.float32) * width
    if len(cuts) > 0:
        array = levels(own_key, dims, cuts, -0.22, 0.18) * array
    return jnp.clip(array, min=-bound, max=bound).astype(held_as)


def gaussian_with(rng, dims, spread, bound, pieces, heavy, kind=jnp.bfloat16):
    values = spread * jax.random.normal(rng, dims, jnp.float32)
    if pieces:
        values = values * levels(rng, dims, pieces, -0.22, 0.18)
    return jnp.clip(with_spikes(values, jax.random.fold_in(rng, 3), *heavy), -bound, bound).astype(kind)


def setup_inputs(seed: int = 0) -> dict:
    key_list = jax.random.split(jax.random.key(seed), 12)
    inputs = scatter_about(key_list[0], (TOKENS, D), 1.0, 6.0, ((0, 32),))
    lengths = draw_lengths(jax.random.fold_in(key_list[11], 71), 0)
    query_weight = scatter_about(key_list[2], (D, D), D ** -0.5, 0.1875, ((1, 32),))
    key_weight = scatter_about(key_list[3], (D, D), D ** -0.5, 0.1875, ((1, 32),))
    value_weight = scatter_about(key_list[4], (D, D), D ** -0.5, 0.1875, ((1, 32),))
    gate_weight = scatter_about(key_list[5], (D, D), D ** -0.5, 0.1875, ((1, 32),))
    out_weight = scatter_about(key_list[6], (D, D), D ** -0.5, 0.1875, ((1, 32),))
    first_weight = scatter_about(key_list[7], (D, FF), D ** -0.5, 0.1875, ((1, 32),))
    second_weight = scatter_about(key_list[8], (D, FF), D ** -0.5, 0.1875, ((1, 32),))
    down_weight = scatter_about(key_list[9], (FF, D), FF ** -0.5, 0.109375, ((1, 32),))
    cotangent = gaussian_with(key_list[10], (TOKENS, D), 1.0, 6.0, ((0, 32),), (0, 1, 32, 2.75))
    return dict(inputs=inputs, lengths=lengths, query_weight=query_weight, key_weight=key_weight, value_weight=value_weight, gate_weight=gate_weight, out_weight=out_weight, first_weight=first_weight, second_weight=second_weight, down_weight=down_weight, cotangent=cotangent)


@jax.custom_vjp
def low(v):
    return lax.optimization_barrier(v.astype(jnp.bfloat16)).astype(jnp.float32)

@jax.custom_vjp
def low_back(v):
    return v

def low_keep(v):
    return (low(v), None)

def low_pass(kept, grad):
    return (grad,)

def back_keep(v):
    return (v, None)

def back_low(kept, grad):
    return (low(grad),)
low.defvjp(low_keep, low_pass)
low_back.defvjp(back_keep, back_low)
NORM_EPS = 1e-06
HIGH = lax.Precision.HIGHEST

def simple_norm(values):
    return values * lax.rsqrt(lax.optimization_barrier(jnp.mean(values * values, axis=-1, keepdims=True)) + NORM_EPS)

def product(left, right):
    return jnp.dot(left, right, precision=HIGH, preferred_element_type=jnp.float32)

def make_tables(length):
    head_index = jnp.arange(HEADS, dtype=jnp.float32)
    slopes = jnp.exp2(-8.0 * (head_index + 1.0) / HEADS) * (1.0 - LAYER / LAYERS)
    offsets = jnp.arange(SPAN, dtype=jnp.float32)
    distance = offsets[:, None] - offsets[None, :]
    within = jnp.where(distance[None] >= 0.0, jnp.exp(-slopes[:, None, None] * jnp.maximum(distance, 0.0)[None]), 0.0)
    query_decay = jnp.exp(-(offsets[:, None] + 1.0) * slopes[None, :])
    key_decay = jnp.exp(-(SPAN - 1.0 - offsets[:, None]) * slopes[None, :])
    block_decay = jnp.exp(-SPAN * slopes)
    places = jnp.arange(length, dtype=jnp.float32)
    frequency = jnp.exp(-jnp.arange(HEAD, dtype=jnp.float32) * (math.log(10000.0) / HEAD))
    angles = places[:, None] * frequency[None, :]
    return (jnp.cos(angles), jnp.sin(angles), within, query_decay, key_decay, block_decay)

def rotate(values, cosine_table, sine_table):
    split_heads = values.reshape(values.shape[0], HEADS, HEAD)
    return jnp.concatenate([split_heads * cosine_table[:, None, :], split_heads * sine_table[:, None, :]], axis=-1)

def lightning(query_rot, key_rot, values, tables):
    cosine_table, sine_table, within, query_decay, key_decay, block_decay = tables
    blocks = query_rot.shape[0] // SPAN
    query_blocks = query_rot.reshape(blocks, SPAN, HEADS, 2 * HEAD)
    key_blocks = key_rot.reshape(blocks, SPAN, HEADS, 2 * HEAD)
    value_blocks = values.reshape(blocks, SPAN, HEADS, HEAD)
    scores = low_back(jnp.einsum('cthf,cshf->chts', query_blocks, key_blocks, precision=HIGH)) * within[None]
    weights_low = low(scores)
    local_part = jnp.einsum('chts,cshe->cthe', weights_low, value_blocks, precision=HIGH)
    query_scaled = low(query_blocks * query_decay[None, :, :, None])
    key_scaled = low(key_blocks * key_decay[None, :, :, None])
    updates = jnp.einsum('cshf,cshe->chfe', key_scaled, value_blocks, precision=HIGH)

    def advance(state, update):
        return (low_back(block_decay[:, None, None] * state + update), state)
    unused, states = lax.scan(advance, jnp.zeros(updates.shape[1:], jnp.float32), updates)
    carried = jnp.einsum('cthf,chfe->cthe', query_scaled, low(states), precision=HIGH)
    return (local_part + carried).reshape(query_rot.shape[0], D)

def layer(inputs_f, weights, mask, tables):
    query_weight, key_weight, value_weight, gate_weight, out_weight, first_weight, second_weight, down_weight = weights
    normed = low(simple_norm(inputs_f))
    query_pre = low_back(product(normed, query_weight))
    key_pre = low_back(product(normed, key_weight))
    value_pre = low_back(product(normed, value_weight))
    gate_pre = low_back(product(normed, gate_weight))
    query_rot = low(rotate(jax.nn.silu(query_pre) * mask, tables[0], tables[1]))
    key_rot = low(rotate(jax.nn.silu(key_pre) * mask, tables[0], tables[1]))
    values = low(value_pre * mask)
    attended = low_back(lightning(query_rot, key_rot, values, tables))
    gated = low(simple_norm(attended) * gate_pre * mask)
    mixed = inputs_f + low_back(product(gated, out_weight))
    normed_two = low(simple_norm(mixed))
    first = low_back(product(normed_two, first_weight))
    second = low_back(product(normed_two, second_weight))
    product_low = low(first * second * mask)
    return mixed + low_back(product(product_low, down_weight))

def reference(inputs, lengths, query_weight, key_weight, value_weight, gate_weight, out_weight, first_weight, second_weight, down_weight, cotangent):
    weights = tuple((matrix.astype(jnp.float32) for matrix in (query_weight, key_weight, value_weight, gate_weight, out_weight, first_weight, second_weight, down_weight)))
    tables = make_tables(TOK_DEV)
    input_rows = inputs.astype(jnp.float32).reshape(SEQS, TOK_DEV, D)
    grad_rows = cotangent.astype(jnp.float32).reshape(SEQS, TOK_DEV, D)
    positions = jnp.arange(TOK_DEV, dtype=jnp.int32)

    def one_sequence(totals, item):
        sequence, upstream, length = item
        mask = (positions < length).astype(jnp.float32)[:, None]

        def forward(sequence_in, weight_set):
            return layer(sequence_in, weight_set, mask, tables)
        result, pull = jax.vjp(forward, sequence, weights)
        sequence_grad, weight_grads = pull(upstream)
        totals = tuple((total + term for total, term in zip(totals, weight_grads)))
        return (totals, (result, sequence_grad))
    initial = tuple((jnp.zeros_like(matrix) for matrix in weights))
    grads, (results, input_grads) = lax.scan(one_sequence, initial, (input_rows, grad_rows, lengths))
    return (results.reshape(TOKENS, D).astype(jnp.bfloat16), input_grads.reshape(TOKENS, D), grads[0], grads[1], grads[2], grads[3], grads[4], grads[5], grads[6], grads[7])
```

```python
import math

import jax
import jax.numpy as jnp
from jax import lax
from jax.sharding import PartitionSpec as P

D = 1024
HEADS = 8
HEAD = 128
SPAN = 256
LAYER = 12
LAYERS = 24


NORM_EPS = 1e-06


def simple_norm(values):
    return values * lax.rsqrt(jnp.mean(values * values, axis=-1, keepdims=True) + NORM_EPS)


def norm_back(values, upstream):
    return jax.vjp(simple_norm, values)[1](upstream)[0]


def silu_back(values, upstream):
    return jax.vjp(jax.nn.silu, values)[1](upstream)[0]


def forward_dot(left, right):
    return jnp.dot(left, right, preferred_element_type=jnp.float32)


def back_dot(left, right):
    return lax.dot_general(
        left, right, (((1,), (1,)), ((), ())), preferred_element_type=jnp.float32
    )


def weight_dot(left, right):
    return lax.dot_general(
        left, right, (((0,), (0,)), ((), ())), preferred_element_type=jnp.float32
    )


def group_columns(lows, shards):
    tokens = lows[0].shape[0]
    width = lows[0].shape[1] // shards
    stacked = jnp.stack([matrix.reshape(tokens, shards, width) for matrix in lows], axis=2)
    return stacked.reshape(tokens, shards * len(lows) * width)


def split_rows(summed, count):
    width = summed.shape[0] // count
    pieces = summed.reshape(count, width, summed.shape[1])
    return tuple((jnp.transpose(pieces[index]) for index in range(count)))


def make_tables(length):
    head_index = jnp.arange(HEADS, dtype=jnp.float32)
    slopes = jnp.exp2(-8.0 * (head_index + 1.0) / HEADS) * (1.0 - LAYER / LAYERS)
    offsets = jnp.arange(SPAN, dtype=jnp.float32)
    distance = offsets[:, None] - offsets[None, :]
    within = jnp.where(
        distance[None] >= 0.0,
        jnp.exp(-slopes[:, None, None] * jnp.maximum(distance, 0.0)[None]),
        0.0,
    )
    query_decay = jnp.exp(-(offsets[:, None] + 1.0) * slopes[None, :])
    key_decay = jnp.exp(-(SPAN - 1.0 - offsets[:, None]) * slopes[None, :])
    block_decay = jnp.exp(-SPAN * slopes)
    places = jnp.arange(length, dtype=jnp.float32)
    frequency = jnp.exp(-jnp.arange(HEAD, dtype=jnp.float32) * (math.log(10000.0) / HEAD))
    angles = places[:, None] * frequency[None, :]
    return (jnp.cos(angles), jnp.sin(angles), within, query_decay, key_decay, block_decay)


def rotate(values, cosine_table, sine_table):
    split_heads = values.reshape(values.shape[0], HEADS, HEAD)
    return jnp.concatenate(
        [split_heads * cosine_table[:, None, :], split_heads * sine_table[:, None, :]], axis=-1
    )


def unrotate(grads, cosine_table, sine_table):
    joined = (
        grads[..., :HEAD] * cosine_table[:, None, :] + grads[..., HEAD:] * sine_table[:, None, :]
    )
    return joined.reshape(grads.shape[0], D)


def lightning_forward(query_rot, key_rot, values, tables):
    cosine_table, sine_table, within, query_decay, key_decay, block_decay = tables
    blocks = query_rot.shape[0] // SPAN
    query_blocks = query_rot.reshape(blocks, SPAN, HEADS, 2 * HEAD)
    key_blocks = key_rot.reshape(blocks, SPAN, HEADS, 2 * HEAD)
    value_blocks = values.reshape(blocks, SPAN, HEADS, HEAD)
    scores = jnp.einsum(
        "cthf,cshf->chts", query_blocks, key_blocks, preferred_element_type=jnp.float32
    )
    weights_low = (scores * within[None]).astype(jnp.bfloat16)
    local_part = jnp.einsum(
        "chts,cshe->cthe", weights_low, value_blocks, preferred_element_type=jnp.float32
    )
    query_scaled = (query_blocks * query_decay[None, :, :, None]).astype(jnp.bfloat16)
    key_scaled = (key_blocks * key_decay[None, :, :, None]).astype(jnp.bfloat16)
    updates = jnp.einsum(
        "cshf,cshe->chfe", key_scaled, value_blocks, preferred_element_type=jnp.float32
    )

    def advance(state, update):
        return (block_decay[:, None, None] * state + update, state)

    unused, states = lax.scan(advance, jnp.zeros(updates.shape[1:], jnp.float32), updates)
    states_low = states.astype(jnp.bfloat16)
    carried = jnp.einsum(
        "cthf,chfe->cthe", query_scaled, states_low, preferred_element_type=jnp.float32
    )
    attended = (local_part + carried).reshape(query_rot.shape[0], D)
    return (attended, (weights_low, query_scaled, key_scaled, states_low))


def lightning_backward(upstream, query_rot, key_rot, values, saved, tables):
    cosine_table, sine_table, within, query_decay, key_decay, block_decay = tables
    weights_low, query_scaled, key_scaled, states_low = saved
    length = query_rot.shape[0]
    blocks = length // SPAN
    query_blocks = query_rot.reshape(blocks, SPAN, HEADS, 2 * HEAD)
    key_blocks = key_rot.reshape(blocks, SPAN, HEADS, 2 * HEAD)
    value_blocks = values.reshape(blocks, SPAN, HEADS, HEAD)
    upstream_blocks = upstream.reshape(blocks, SPAN, HEADS, HEAD)
    weight_grad = jnp.einsum(
        "cthe,cshe->chts", upstream_blocks, value_blocks, preferred_element_type=jnp.float32
    )
    score_low = (weight_grad * within[None]).astype(jnp.bfloat16)
    query_part = jnp.einsum(
        "chts,cshf->cthf", score_low, key_blocks, preferred_element_type=jnp.float32
    )
    key_part = jnp.einsum(
        "chts,cthf->cshf", score_low, query_blocks, preferred_element_type=jnp.float32
    )
    value_part = jnp.einsum(
        "chts,cthe->cshe", weights_low, upstream_blocks, preferred_element_type=jnp.float32
    )
    scaled_grad = jnp.einsum(
        "cthe,chfe->cthf", upstream_blocks, states_low, preferred_element_type=jnp.float32
    )
    query_part = query_part + scaled_grad * query_decay[None, :, :, None]
    state_terms = jnp.einsum(
        "cthf,cthe->chfe", query_scaled, upstream_blocks, preferred_element_type=jnp.float32
    )

    def retreat(later, term):
        return (
            (block_decay[:, None, None] * later.astype(jnp.float32) + term).astype(jnp.bfloat16),
            later,
        )

    unused, update_grads = lax.scan(
        retreat, jnp.zeros(state_terms.shape[1:], jnp.bfloat16), state_terms, reverse=True
    )
    key_scaled_grad = jnp.einsum(
        "cshe,chfe->cshf", value_blocks, update_grads, preferred_element_type=jnp.float32
    )
    key_part = key_part + key_scaled_grad * key_decay[None, :, :, None]
    value_part = value_part + jnp.einsum(
        "cshf,chfe->cshe", key_scaled, update_grads, preferred_element_type=jnp.float32
    )
    return (
        query_part.reshape(length, HEADS, 2 * HEAD),
        key_part.reshape(length, HEADS, 2 * HEAD),
        value_part.reshape(length, D),
    )


def attention_forward(inputs_f, mask, weights, tables):
    query_weight, key_weight, value_weight, gate_weight, out_weight = weights
    normed = simple_norm(inputs_f).astype(jnp.bfloat16)
    query_pre = forward_dot(normed, query_weight)
    key_pre = forward_dot(normed, key_weight)
    value_pre = forward_dot(normed, value_weight)
    gate_pre = forward_dot(normed, gate_weight)
    query_rot = rotate(jax.nn.silu(query_pre) * mask, tables[0], tables[1]).astype(jnp.bfloat16)
    key_rot = rotate(jax.nn.silu(key_pre) * mask, tables[0], tables[1]).astype(jnp.bfloat16)
    values = (value_pre * mask).astype(jnp.bfloat16)
    attended, saved = lightning_forward(query_rot, key_rot, values, tables)
    attended_norm = simple_norm(attended)
    gated = (attended_norm * gate_pre * mask).astype(jnp.bfloat16)
    mixed = inputs_f + forward_dot(gated, out_weight)
    kept = (
        normed,
        query_pre,
        key_pre,
        gate_pre,
        values,
        query_rot,
        key_rot,
        attended,
        attended_norm,
        gated,
        saved,
    )
    return (mixed, kept)


def glu_forward(mixed, mask, weights):
    first_weight, second_weight, down_weight = weights
    normed_two = simple_norm(mixed).astype(jnp.bfloat16)
    first = forward_dot(normed_two, first_weight)
    second = forward_dot(normed_two, second_weight)
    product_low = (first * second * mask).astype(jnp.bfloat16)
    result = mixed + forward_dot(product_low, down_weight)
    return (result, (normed_two, first, second, product_low))


AXES = ("dp", "fsdp")
ROWS = 24


def gather_rows(matrices, shards):
    count = len(matrices)
    local = jnp.stack([jnp.transpose(matrix).reshape(-1, D) for matrix in matrices])
    width = local.shape[1]
    full = lax.all_gather(local.reshape(count * width, D), AXES, axis=0, tiled=True)
    full = full.reshape(shards, count, width, D)
    return tuple(full[:, index].reshape(shards * width, D) for index in range(count))


def scatter_rows(terms, shards):
    count = len(terms)
    width = terms[0].shape[0] // shards
    extra = -count * width % ROWS
    pieces = [term.reshape(shards, width, D) for term in terms]
    if extra:
        pieces.append(jnp.zeros((shards, extra, D), terms[0].dtype))
    stacked = jnp.concatenate(pieces, axis=1)
    summed = lax.psum_scatter(
        stacked.reshape(shards * (count * width + extra), D), AXES, scatter_dimension=0, tiled=True
    )
    return summed[: count * width].reshape(count, width, D)


def weight_term(left, right):
    return weight_dot(left, right).astype(jnp.bfloat16)


def per_device(
    inputs,
    lengths,
    query_weight,
    key_weight,
    value_weight,
    gate_weight,
    out_weight,
    first_weight,
    second_weight,
    down_weight,
    cotangent,
):
    shards = lax.axis_size(AXES)
    query_t, key_t, value_t, gate_t, out_t = gather_rows(
        (query_weight, key_weight, value_weight, gate_weight, out_weight), shards
    )
    first_t, second_t, down_flat = gather_rows((first_weight, second_weight, down_weight), shards)
    down_t = down_flat.reshape(D, -1)
    inputs_f = inputs.astype(jnp.float32)
    length = inputs.shape[0]
    mask = (lax.iota(jnp.int32, length) < lengths[0]).astype(jnp.float32)[:, None]
    tables = make_tables(length)
    normed = simple_norm(inputs_f).astype(jnp.bfloat16)
    query_pre = back_dot(normed, query_t)
    key_pre = back_dot(normed, key_t)
    value_pre = back_dot(normed, value_t)
    gate_pre = back_dot(normed, gate_t)
    query_rot = rotate(jax.nn.silu(query_pre) * mask, tables[0], tables[1]).astype(jnp.bfloat16)
    key_rot = rotate(jax.nn.silu(key_pre) * mask, tables[0], tables[1]).astype(jnp.bfloat16)
    values = (value_pre * mask).astype(jnp.bfloat16)
    attended, saved = lightning_forward(query_rot, key_rot, values, tables)
    attended_norm = simple_norm(attended)
    gated = (attended_norm * gate_pre * mask).astype(jnp.bfloat16)
    mixed = inputs_f + back_dot(gated, out_t)
    normed_two = simple_norm(mixed).astype(jnp.bfloat16)
    first = back_dot(normed_two, first_t)
    second = back_dot(normed_two, second_t)
    product_low = (first * second * mask).astype(jnp.bfloat16)
    result = mixed + back_dot(product_low, down_t)
    product_grad = forward_dot(cotangent, down_t)
    first_low = (product_grad * second * mask).astype(jnp.bfloat16)
    second_low = (product_grad * first * mask).astype(jnp.bfloat16)
    normed_two_grad = forward_dot(first_low, first_t) + forward_dot(second_low, second_t)
    down_term = weight_term(cotangent, product_low).reshape(-1, D)
    glu_sums = scatter_rows(
        (weight_term(first_low, normed_two), weight_term(second_low, normed_two), down_term),
        shards,
    ).astype(jnp.float32)
    first_sum = jnp.transpose(glu_sums[0])
    second_sum = jnp.transpose(glu_sums[1])
    down_sum = jnp.transpose(glu_sums[2].reshape(down_weight.shape[1], -1))
    mixed_grad = cotangent.astype(jnp.float32) + norm_back(mixed, normed_two_grad)
    mixed_low = mixed_grad.astype(jnp.bfloat16)
    gated_grad = forward_dot(mixed_low, out_t)
    gate_low = (gated_grad * attended_norm * mask).astype(jnp.bfloat16)
    attended_low = norm_back(attended, gated_grad * gate_pre * mask).astype(jnp.bfloat16)
    query_rot_grad, key_rot_grad, values_grad = lightning_backward(
        attended_low, query_rot, key_rot, values, saved, tables
    )
    query_low = silu_back(query_pre, unrotate(query_rot_grad, tables[0], tables[1]) * mask).astype(
        jnp.bfloat16
    )
    key_low = silu_back(key_pre, unrotate(key_rot_grad, tables[0], tables[1]) * mask).astype(
        jnp.bfloat16
    )
    value_low = (values_grad * mask).astype(jnp.bfloat16)
    attn_sums = scatter_rows(
        (
            weight_term(query_low, normed),
            weight_term(key_low, normed),
            weight_term(value_low, normed),
            weight_term(gate_low, normed),
            weight_term(mixed_low, gated),
        ),
        shards,
    ).astype(jnp.float32)
    normed_grad = (
        forward_dot(query_low, query_t)
        + forward_dot(key_low, key_t)
        + forward_dot(value_low, value_t)
        + forward_dot(gate_low, gate_t)
    )
    input_grad = mixed_grad + norm_back(inputs_f, normed_grad)
    query_sum, key_sum, value_sum, gate_sum, out_sum = (
        jnp.transpose(attn_sums[index]) for index in range(5)
    )
    return (
        result.astype(jnp.bfloat16),
        input_grad,
        query_sum,
        key_sum,
        value_sum,
        gate_sum,
        out_sum,
        first_sum,
        second_sum,
        down_sum,
    )


def solution(mesh):
    return jax.shard_map(
        per_device,
        mesh=mesh,
        in_specs=(
            P(("dp", "fsdp"), None),
            P(("dp", "fsdp")),
            P(None, ("dp", "fsdp")),
            P(None, ("dp", "fsdp")),
            P(None, ("dp", "fsdp")),
            P(None, ("dp", "fsdp")),
            P(None, ("dp", "fsdp")),
            P(None, ("dp", "fsdp")),
            P(None, ("dp", "fsdp")),
            P(None, ("dp", "fsdp")),
            P(("dp", "fsdp"), None),
        ),
        out_specs=(
            P(("dp", "fsdp"), None),
            P(("dp", "fsdp"), None),
            P(None, ("dp", "fsdp")),
            P(None, ("dp", "fsdp")),
            P(None, ("dp", "fsdp")),
            P(None, ("dp", "fsdp")),
            P(None, ("dp", "fsdp")),
            P(None, ("dp", "fsdp")),
            P(None, ("dp", "fsdp")),
            P(None, ("dp", "fsdp")),
        ),
        check_vma=False,
    )
```

```python
import math

import jax
import jax.numpy as jnp
from jax import lax
from jax.sharding import PartitionSpec as P

D = 1024
HEADS = 8
HEAD = 128
SPAN = 256
LAYER = 12
LAYERS = 24


NORM_EPS = 1e-06


def simple_norm(values):
    return values * lax.rsqrt(jnp.mean(values * values, axis=-1, keepdims=True) + NORM_EPS)


def norm_back(values, upstream):
    return jax.vjp(simple_norm, values)[1](upstream)[0]


def silu_back(values, upstream):
    return jax.vjp(jax.nn.silu, values)[1](upstream)[0]


def forward_dot(left, right):
    return jnp.dot(left, right, preferred_element_type=jnp.float32)


def back_dot(left, right):
    return lax.dot_general(
        left, right, (((1,), (1,)), ((), ())), preferred_element_type=jnp.float32
    )


def weight_dot(left, right):
    return lax.dot_general(
        left, right, (((0,), (0,)), ((), ())), preferred_element_type=jnp.float32
    )


def group_columns(lows, shards):
    tokens = lows[0].shape[0]
    width = lows[0].shape[1] // shards
    stacked = jnp.stack([matrix.reshape(tokens, shards, width) for matrix in lows], axis=2)
    return stacked.reshape(tokens, shards * len(lows) * width)


def split_rows(summed, count):
    width = summed.shape[0] // count
    pieces = summed.reshape(count, width, summed.shape[1])
    return tuple((jnp.transpose(pieces[index]) for index in range(count)))


def make_tables(length):
    head_index = jnp.arange(HEADS, dtype=jnp.float32)
    slopes = jnp.exp2(-8.0 * (head_index + 1.0) / HEADS) * (1.0 - LAYER / LAYERS)
    offsets = jnp.arange(SPAN, dtype=jnp.float32)
    distance = offsets[:, None] - offsets[None, :]
    within = jnp.where(
        distance[None] >= 0.0,
        jnp.exp(-slopes[:, None, None] * jnp.maximum(distance, 0.0)[None]),
        0.0,
    )
    query_decay = jnp.exp(-(offsets[:, None] + 1.0) * slopes[None, :])
    key_decay = jnp.exp(-(SPAN - 1.0 - offsets[:, None]) * slopes[None, :])
    block_decay = jnp.exp(-SPAN * slopes)
    places = jnp.arange(length, dtype=jnp.float32)
    frequency = jnp.exp(-jnp.arange(HEAD, dtype=jnp.float32) * (math.log(10000.0) / HEAD))
    angles = places[:, None] * frequency[None, :]
    return (jnp.cos(angles), jnp.sin(angles), within, query_decay, key_decay, block_decay)


def rotate(values, cosine_table, sine_table):
    split_heads = values.reshape(values.shape[0], HEADS, HEAD)
    return jnp.concatenate(
        [split_heads * cosine_table[:, None, :], split_heads * sine_table[:, None, :]], axis=-1
    )


def unrotate(grads, cosine_table, sine_table):
    joined = (
        grads[..., :HEAD] * cosine_table[:, None, :] + grads[..., HEAD:] * sine_table[:, None, :]
    )
    return joined.reshape(grads.shape[0], D)


def lightning_forward(query_rot, key_rot, values, tables):
    cosine_table, sine_table, within, query_decay, key_decay, block_decay = tables
    blocks = query_rot.shape[0] // SPAN
    query_blocks = query_rot.reshape(blocks, SPAN, HEADS, 2 * HEAD)
    key_blocks = key_rot.reshape(blocks, SPAN, HEADS, 2 * HEAD)
    value_blocks = values.reshape(blocks, SPAN, HEADS, HEAD)
    scores = jnp.einsum(
        "cthf,cshf->chts", query_blocks, key_blocks, preferred_element_type=jnp.float32
    )
    weights_low = (scores * within[None]).astype(jnp.bfloat16)
    local_part = jnp.einsum(
        "chts,cshe->cthe", weights_low, value_blocks, preferred_element_type=jnp.float32
    )
    query_scaled = (query_blocks * query_decay[None, :, :, None]).astype(jnp.bfloat16)
    key_scaled = (key_blocks * key_decay[None, :, :, None]).astype(jnp.bfloat16)
    updates = jnp.einsum(
        "cshf,cshe->chfe", key_scaled, value_blocks, preferred_element_type=jnp.float32
    )

    def advance(state, update):
        return (block_decay[:, None, None] * state + update, state)

    unused, states = lax.scan(advance, jnp.zeros(updates.shape[1:], jnp.float32), updates)
    states_low = states.astype(jnp.bfloat16)
    carried = jnp.einsum(
        "cthf,chfe->cthe", query_scaled, states_low, preferred_element_type=jnp.float32
    )
    attended = (local_part + carried).reshape(query_rot.shape[0], D)
    return (attended, (weights_low, query_scaled, key_scaled, states_low))


def lightning_backward(upstream, query_rot, key_rot, values, saved, tables):
    cosine_table, sine_table, within, query_decay, key_decay, block_decay = tables
    weights_low, query_scaled, key_scaled, states_low = saved
    length = query_rot.shape[0]
    blocks = length // SPAN
    query_blocks = query_rot.reshape(blocks, SPAN, HEADS, 2 * HEAD)
    key_blocks = key_rot.reshape(blocks, SPAN, HEADS, 2 * HEAD)
    value_blocks = values.reshape(blocks, SPAN, HEADS, HEAD)
    upstream_blocks = upstream.reshape(blocks, SPAN, HEADS, HEAD)
    weight_grad = jnp.einsum(
        "cthe,cshe->chts", upstream_blocks, value_blocks, preferred_element_type=jnp.float32
    )
    score_low = (weight_grad * within[None]).astype(jnp.bfloat16)
    query_part = jnp.einsum(
        "chts,cshf->cthf", score_low, key_blocks, preferred_element_type=jnp.float32
    )
    key_part = jnp.einsum(
        "chts,cthf->cshf", score_low, query_blocks, preferred_element_type=jnp.float32
    )
    value_part = jnp.einsum(
        "chts,cthe->cshe", weights_low, upstream_blocks, preferred_element_type=jnp.float32
    )
    scaled_grad = jnp.einsum(
        "cthe,chfe->cthf", upstream_blocks, states_low, preferred_element_type=jnp.float32
    )
    query_part = query_part + scaled_grad * query_decay[None, :, :, None]
    state_terms = jnp.einsum(
        "cthf,cthe->chfe", query_scaled, upstream_blocks, preferred_element_type=jnp.float32
    )

    def retreat(later, term):
        return (
            (block_decay[:, None, None] * later.astype(jnp.float32) + term).astype(jnp.bfloat16),
            later,
        )

    unused, update_grads = lax.scan(
        retreat, jnp.zeros(state_terms.shape[1:], jnp.bfloat16), state_terms, reverse=True
    )
    key_scaled_grad = jnp.einsum(
        "cshe,chfe->cshf", value_blocks, update_grads, preferred_element_type=jnp.float32
    )
    key_part = key_part + key_scaled_grad * key_decay[None, :, :, None]
    value_part = value_part + jnp.einsum(
        "cshf,chfe->cshe", key_scaled, update_grads, preferred_element_type=jnp.float32
    )
    return (
        query_part.reshape(length, HEADS, 2 * HEAD),
        key_part.reshape(length, HEADS, 2 * HEAD),
        value_part.reshape(length, D),
    )


def attention_forward(inputs_f, mask, weights, tables):
    query_weight, key_weight, value_weight, gate_weight, out_weight = weights
    normed = simple_norm(inputs_f).astype(jnp.bfloat16)
    query_pre = forward_dot(normed, query_weight)
    key_pre = forward_dot(normed, key_weight)
    value_pre = forward_dot(normed, value_weight)
    gate_pre = forward_dot(normed, gate_weight)
    query_rot = rotate(jax.nn.silu(query_pre) * mask, tables[0], tables[1]).astype(jnp.bfloat16)
    key_rot = rotate(jax.nn.silu(key_pre) * mask, tables[0], tables[1]).astype(jnp.bfloat16)
    values = (value_pre * mask).astype(jnp.bfloat16)
    attended, saved = lightning_forward(query_rot, key_rot, values, tables)
    attended_norm = simple_norm(attended)
    gated = (attended_norm * gate_pre * mask).astype(jnp.bfloat16)
    mixed = inputs_f + forward_dot(gated, out_weight)
    kept = (
        normed,
        query_pre,
        key_pre,
        gate_pre,
        values,
        query_rot,
        key_rot,
        attended,
        attended_norm,
        gated,
        saved,
    )
    return (mixed, kept)


def glu_forward(mixed, mask, weights):
    first_weight, second_weight, down_weight = weights
    normed_two = simple_norm(mixed).astype(jnp.bfloat16)
    first = forward_dot(normed_two, first_weight)
    second = forward_dot(normed_two, second_weight)
    product_low = (first * second * mask).astype(jnp.bfloat16)
    result = mixed + forward_dot(product_low, down_weight)
    return (result, (normed_two, first, second, product_low))


AXES = ("dp", "fsdp")


def gather_rows(matrices, shards):
    count = len(matrices)
    local = jnp.stack([jnp.transpose(matrix).reshape(-1, D) for matrix in matrices])
    width = local.shape[1]
    full = lax.all_gather(local.reshape(count * width, D), AXES, axis=0, tiled=True)
    full = full.reshape(shards, count, width, D)
    return tuple(full[:, index].reshape(shards * width, D) for index in range(count))


def pick(parts, axis, index):
    return lax.dynamic_index_in_dim(parts, index, axis, keepdims=False)


def add_low(*pieces):
    total = pieces[0].astype(jnp.float32)
    for piece in pieces[1:]:
        total = total + piece.astype(jnp.float32)
    return total.astype(jnp.bfloat16)


class Line:
    def __init__(self, name, size, inner):
        self.name, self.size, self.inner = name, size, inner
        self.place = lax.axis_index(name) // inner % size

    def move(self, value, shift, allowed):
        pairs = []
        for source in range(lax.axis_size(self.name)):
            place = source // self.inner % self.size
            if place in allowed and 0 <= place + shift < self.size:
                pairs.append((source, source + shift * self.inner))
        return lax.ppermute(value, self.name, pairs)

    def swap(self, value):
        pairs = []
        for source in range(lax.axis_size(self.name)):
            place = source // self.inner % self.size
            pairs.append((source, source + (1 - 2 * place) * self.inner))
        return lax.ppermute(value, self.name, pairs)

    def scatter(self, parts, axis):
        size = self.size
        if size == 1:
            return pick(parts, axis, 0)
        own = pick(parts, axis, self.place)
        if size == 2:
            return add_low(own, self.swap(pick(parts, axis, 1 - self.place)))
        rising = pick(parts, axis, jnp.minimum(self.place + size - 1, size - 1))
        falling = pick(parts, axis, jnp.maximum(self.place - size + 1, 0))
        for step in range(1, size):
            rising = self.move(rising, 1, range(step))
            falling = self.move(falling, -1, range(size - step, size))
            if step < size - 1:
                up = jnp.minimum(self.place + size - step - 1, size - 1)
                down = jnp.maximum(self.place - size + step + 1, 0)
                rising = add_low(pick(parts, axis, up), rising)
                falling = add_low(pick(parts, axis, down), falling)
        return add_low(own, rising, falling)


def lines():
    rows = lax.axis_size("dp")
    columns = lax.axis_size("fsdp")
    short = 1 << ((columns.bit_length() - 1) // 2)
    return (
        Line("dp", 2, 1),
        Line("dp", rows // 2, 2),
        Line("fsdp", short, 1),
        Line("fsdp", columns // short, short),
    )


def scatter_rows(terms, shards):
    core, across, up, deep = lines()
    width = terms[0].shape[0] // shards
    half = D // 2
    parts = jnp.stack(
        [
            term.reshape(across.size, 2, deep.size, up.size, width, D)
            for term in terms
        ]
    )
    parts = core.scatter(parts, 2)
    left = up.scatter(across.scatter(parts[..., :half], 1), 2)
    right = across.scatter(up.scatter(parts[..., half:], 3), 1)
    return deep.scatter(jnp.concatenate([left, right], axis=-1), 1)


def weight_term(left, right):
    return weight_dot(left, right).astype(jnp.bfloat16)


def per_device(
    inputs,
    lengths,
    query_weight,
    key_weight,
    value_weight,
    gate_weight,
    out_weight,
    first_weight,
    second_weight,
    down_weight,
    cotangent,
):
    shards = lax.axis_size(AXES)
    query_t, key_t, value_t, gate_t, out_t = gather_rows(
        (query_weight, key_weight, value_weight, gate_weight, out_weight), shards
    )
    first_t, second_t, down_flat = gather_rows((first_weight, second_weight, down_weight), shards)
    down_t = down_flat.reshape(D, -1)
    inputs_f = inputs.astype(jnp.float32)
    length = inputs.shape[0]
    mask = (lax.iota(jnp.int32, length) < lengths[0]).astype(jnp.float32)[:, None]
    tables = make_tables(length)
    normed = simple_norm(inputs_f).astype(jnp.bfloat16)
    query_pre = back_dot(normed, query_t)
    key_pre = back_dot(normed, key_t)
    value_pre = back_dot(normed, value_t)
    gate_pre = back_dot(normed, gate_t)
    query_rot = rotate(jax.nn.silu(query_pre) * mask, tables[0], tables[1]).astype(jnp.bfloat16)
    key_rot = rotate(jax.nn.silu(key_pre) * mask, tables[0], tables[1]).astype(jnp.bfloat16)
    values = (value_pre * mask).astype(jnp.bfloat16)
    attended, saved = lightning_forward(query_rot, key_rot, values, tables)
    attended_norm = simple_norm(attended)
    gated = (attended_norm * gate_pre * mask).astype(jnp.bfloat16)
    mixed = inputs_f + back_dot(gated, out_t)
    normed_two = simple_norm(mixed).astype(jnp.bfloat16)
    first = back_dot(normed_two, first_t)
    second = back_dot(normed_two, second_t)
    product_low = (first * second * mask).astype(jnp.bfloat16)
    result = mixed + back_dot(product_low, down_t)
    product_grad = forward_dot(cotangent, down_t)
    first_low = (product_grad * second * mask).astype(jnp.bfloat16)
    second_low = (product_grad * first * mask).astype(jnp.bfloat16)
    normed_two_grad = forward_dot(first_low, first_t) + forward_dot(second_low, second_t)
    down_term = weight_term(cotangent, product_low).reshape(-1, D)
    glu_sums = scatter_rows(
        (weight_term(first_low, normed_two), weight_term(second_low, normed_two), down_term),
        shards,
    ).astype(jnp.float32)
    first_sum = jnp.transpose(glu_sums[0])
    second_sum = jnp.transpose(glu_sums[1])
    down_sum = jnp.transpose(glu_sums[2].reshape(down_weight.shape[1], -1))
    mixed_grad = cotangent.astype(jnp.float32) + norm_back(mixed, normed_two_grad)
    mixed_low = mixed_grad.astype(jnp.bfloat16)
    gated_grad = forward_dot(mixed_low, out_t)
    gate_low = (gated_grad * attended_norm * mask).astype(jnp.bfloat16)
    early_sums = scatter_rows(
        (weight_term(mixed_low, gated), weight_term(gate_low, normed)), shards
    ).astype(jnp.float32)
    attended_low = norm_back(attended, gated_grad * gate_pre * mask).astype(jnp.bfloat16)
    query_rot_grad, key_rot_grad, values_grad = lightning_backward(
        attended_low, query_rot, key_rot, values, saved, tables
    )
    query_low = silu_back(query_pre, unrotate(query_rot_grad, tables[0], tables[1]) * mask).astype(
        jnp.bfloat16
    )
    key_low = silu_back(key_pre, unrotate(key_rot_grad, tables[0], tables[1]) * mask).astype(
        jnp.bfloat16
    )
    value_low = (values_grad * mask).astype(jnp.bfloat16)
    late_sums = scatter_rows(
        (
            weight_term(query_low, normed),
            weight_term(key_low, normed),
            weight_term(value_low, normed),
        ),
        shards,
    ).astype(jnp.float32)
    normed_grad = (
        forward_dot(query_low, query_t)
        + forward_dot(key_low, key_t)
        + forward_dot(value_low, value_t)
        + forward_dot(gate_low, gate_t)
    )
    input_grad = mixed_grad + norm_back(inputs_f, normed_grad)
    query_sum, key_sum, value_sum = (jnp.transpose(late_sums[index]) for index in range(3))
    out_sum, gate_sum = (jnp.transpose(early_sums[index]) for index in range(2))
    return (
        result.astype(jnp.bfloat16),
        input_grad,
        query_sum,
        key_sum,
        value_sum,
        gate_sum,
        out_sum,
        first_sum,
        second_sum,
        down_sum,
    )


def solution(mesh):
    return jax.shard_map(
        per_device,
        mesh=mesh,
        in_specs=(
            P(("dp", "fsdp"), None),
            P(("dp", "fsdp")),
            P(None, ("dp", "fsdp")),
            P(None, ("dp", "fsdp")),
            P(None, ("dp", "fsdp")),
            P(None, ("dp", "fsdp")),
            P(None, ("dp", "fsdp")),
            P(None, ("dp", "fsdp")),
            P(None, ("dp", "fsdp")),
            P(None, ("dp", "fsdp")),
            P(("dp", "fsdp"), None),
        ),
        out_specs=(
            P(("dp", "fsdp"), None),
            P(("dp", "fsdp"), None),
            P(None, ("dp", "fsdp")),
            P(None, ("dp", "fsdp")),
            P(None, ("dp", "fsdp")),
            P(None, ("dp", "fsdp")),
            P(None, ("dp", "fsdp")),
            P(None, ("dp", "fsdp")),
            P(None, ("dp", "fsdp")),
            P(None, ("dp", "fsdp")),
        ),
        check_vma=False,
    )
```

```python
import math

import jax
import jax.numpy as jnp
from jax import lax
from jax.experimental import pallas as pl
from jax.experimental.pallas import tpu as pltpu
from jax.sharding import PartitionSpec as P

D = 1024
HEADS = 8
HEAD = 128
SPAN = 256
LAYER = 12
LAYERS = 24


NORM_EPS = 1e-06


def simple_norm(values):
    return values * lax.rsqrt(jnp.mean(values * values, axis=-1, keepdims=True) + NORM_EPS)


def norm_back(values, upstream):
    return jax.vjp(simple_norm, values)[1](upstream)[0]


def forward_dot(left, right):
    return jnp.dot(left, right, preferred_element_type=jnp.float32)


def back_dot(left, right):
    return lax.dot_general(
        left, right, (((1,), (1,)), ((), ())), preferred_element_type=jnp.float32
    )


def weight_dot(left, right):
    return lax.dot_general(
        left, right, (((0,), (0,)), ((), ())), preferred_element_type=jnp.float32
    )


def make_tables(length):
    head_index = jnp.arange(HEADS, dtype=jnp.float32)
    slopes = jnp.exp2(-8.0 * (head_index + 1.0) / HEADS) * (1.0 - LAYER / LAYERS)
    places = jnp.arange(length, dtype=jnp.float32)
    frequency = jnp.exp(-jnp.arange(HEAD, dtype=jnp.float32) * (math.log(10000.0) / HEAD))
    angles = places[:, None] * frequency[None, :]
    return (jnp.cos(angles), jnp.sin(angles), slopes)


def dot_nn(left, right):
    return lax.dot_general(
        left, right, (((1,), (0,)), ((), ())), preferred_element_type=jnp.float32
    )


def decays(slope):
    rows = lax.broadcasted_iota(jnp.int32, (SPAN, SPAN), 0).astype(jnp.float32)
    columns = lax.broadcasted_iota(jnp.int32, (SPAN, SPAN), 1).astype(jnp.float32)
    distance = rows - columns
    within = jnp.where(distance >= 0.0, jnp.exp(-slope * jnp.maximum(distance, 0.0)), 0.0)
    query_decay = jnp.exp(-(rows + 1.0) * slope)
    key_decay = jnp.exp(-(SPAN - 1.0 - rows) * slope)
    block_decay = jnp.exp(jnp.full((1, HEAD), -SPAN, jnp.float32) * slope)
    return within, query_decay, key_decay, block_decay


def span_rows(block):
    return pl.ds(block * SPAN, SPAN)


def span_mask(block, count):
    places = lax.broadcasted_iota(jnp.int32, (SPAN, HEAD), 0) + block * SPAN
    return (places < count).astype(jnp.float32)


def turned(pre, mask, cosine, sine):
    active = pre * jax.nn.sigmoid(pre) * mask
    return jnp.concatenate([active * cosine, active * sine], axis=-1).astype(jnp.bfloat16)


def scaled(turned_block, decay):
    return (turned_block.astype(jnp.float32) * decay).astype(jnp.bfloat16)


def forward_kernel(count_ref, slope_ref, query_ref, key_ref, value_ref, cosine_ref, sine_ref, out_ref):
    within, query_decay, key_decay, block_decay = decays(slope_ref[pl.program_id(0)])
    state = jnp.zeros((2 * HEAD, HEAD), jnp.float32)
    for block in range(query_ref.shape[0] // SPAN):
        rows = span_rows(block)
        mask = span_mask(block, count_ref[0])
        cosine, sine = cosine_ref[rows, :], sine_ref[rows, :]
        query = turned(query_ref[rows, :], mask, cosine, sine)
        key = turned(key_ref[rows, :], mask, cosine, sine)
        value = (value_ref[rows, :] * mask).astype(jnp.bfloat16)
        weights_low = (back_dot(query, key) * within).astype(jnp.bfloat16)
        out_ref[rows, :] = dot_nn(weights_low, value) + dot_nn(
            scaled(query, query_decay), state.astype(jnp.bfloat16)
        )
        state = block_decay * state + weight_dot(scaled(key, key_decay), value)


def silu_slope(pre):
    gate = jax.nn.sigmoid(pre)
    return gate * (1.0 + pre * (1.0 - gate))


def backward_kernel(
    count_ref,
    slope_ref,
    query_ref,
    key_ref,
    value_ref,
    upstream_ref,
    cosine_ref,
    sine_ref,
    query_low_ref,
    key_low_ref,
    value_low_ref,
    state_ref,
):
    within, query_decay, key_decay, block_decay = decays(slope_ref[pl.program_id(0)])
    blocks = query_ref.shape[0] // SPAN
    state = jnp.zeros((2 * HEAD, HEAD), jnp.float32)
    for block in range(blocks):
        state_ref[block] = state.astype(jnp.bfloat16)
        if block + 1 < blocks:
            rows = span_rows(block)
            mask = span_mask(block, count_ref[0])
            key = turned(key_ref[rows, :], mask, cosine_ref[rows, :], sine_ref[rows, :])
            value = (value_ref[rows, :] * mask).astype(jnp.bfloat16)
            state = block_decay * state + weight_dot(scaled(key, key_decay), value)
    later = jnp.zeros((2 * HEAD, HEAD), jnp.bfloat16)
    for block in reversed(range(blocks)):
        rows = span_rows(block)
        mask = span_mask(block, count_ref[0])
        cosine, sine = cosine_ref[rows, :], sine_ref[rows, :]
        query_pre, key_pre = query_ref[rows, :], key_ref[rows, :]
        query = turned(query_pre, mask, cosine, sine)
        key = turned(key_pre, mask, cosine, sine)
        value = (value_ref[rows, :] * mask).astype(jnp.bfloat16)
        upstream = upstream_ref[rows, :]
        weights_low = (back_dot(query, key) * within).astype(jnp.bfloat16)
        score_low = (back_dot(upstream, value) * within).astype(jnp.bfloat16)
        query_grad = dot_nn(score_low, key) + query_decay * back_dot(upstream, state_ref[block])
        key_grad = weight_dot(score_low, query) + key_decay * back_dot(value, later)
        value_grad = weight_dot(weights_low, upstream) + dot_nn(scaled(key, key_decay), later)
        query_back = (query_grad[:, :HEAD] * cosine + query_grad[:, HEAD:] * sine) * mask
        key_back = (key_grad[:, :HEAD] * cosine + key_grad[:, HEAD:] * sine) * mask
        query_low_ref[rows, :] = (silu_slope(query_pre) * query_back).astype(jnp.bfloat16)
        key_low_ref[rows, :] = (silu_slope(key_pre) * key_back).astype(jnp.bfloat16)
        value_low_ref[rows, :] = (value_grad * mask).astype(jnp.bfloat16)
        if block > 0:
            term = weight_dot(scaled(query, query_decay), upstream)
            later = (block_decay * later.astype(jnp.float32) + term).astype(jnp.bfloat16)


def head_specs(length, count):
    return [pl.BlockSpec((length, HEAD), lambda head: (0, head)) for _ in range(count)]


def shared_specs(length):
    return [pl.BlockSpec((length, HEAD), lambda head: (0, 0)) for _ in range(2)]


def scalar_specs():
    return [pl.BlockSpec(memory_space=pltpu.SMEM) for _ in range(2)]


def lightning_forward(lengths, query_pre, key_pre, value_pre, tables, interpret=False):
    length = query_pre.shape[0]
    return pl.pallas_call(
        forward_kernel,
        grid=(HEADS,),
        in_specs=scalar_specs() + head_specs(length, 3) + shared_specs(length),
        out_specs=head_specs(length, 1)[0],
        out_shape=jax.ShapeDtypeStruct((length, D), jnp.float32),
        name="lightning_forward",
        interpret=interpret,
    )(lengths, tables[2], query_pre, key_pre, value_pre, tables[0], tables[1])


def lightning_backward(lengths, query_pre, key_pre, value_pre, upstream, tables, interpret=False):
    length = query_pre.shape[0]
    return pl.pallas_call(
        backward_kernel,
        grid=(HEADS,),
        in_specs=scalar_specs() + head_specs(length, 4) + shared_specs(length),
        out_specs=head_specs(length, 3),
        out_shape=[jax.ShapeDtypeStruct((length, D), jnp.bfloat16)] * 3,
        scratch_shapes=[pltpu.VMEM((length // SPAN, 2 * HEAD, HEAD), jnp.bfloat16)],
        name="lightning_backward",
        interpret=interpret,
    )(lengths, tables[2], query_pre, key_pre, value_pre, upstream, tables[0], tables[1])


AXES = ("dp", "fsdp")


def lane_rows(matrix):
    extra = -matrix.shape[-1] % D
    if extra:
        matrix = jnp.pad(matrix, [(0, 0)] * (matrix.ndim - 1) + [(0, extra)])
    return jnp.split(matrix, matrix.shape[-1] // D, axis=-1)


def gather_rows(matrices, shards):
    pieces = [piece for matrix in matrices for piece in lane_rows(jnp.transpose(matrix))]
    full = lax.all_gather(jnp.concatenate(pieces, axis=0), AXES, axis=0, tiled=True)
    full = full.reshape(shards, -1, D)
    gathered, start = [], 0
    for matrix in matrices:
        size, width = matrix.shape
        count = -(-size // D)
        columns = [
            full[:, start + index * width : start + (index + 1) * width].reshape(shards * width, D)
            for index in range(count)
        ]
        joined = columns[0] if count == 1 else jnp.concatenate(columns, axis=1)[:, :size]
        gathered.append(joined)
        start += count * width
    return gathered


def pick(parts, axis, index):
    return lax.dynamic_index_in_dim(parts, index, axis, keepdims=False)


def add_low(*pieces):
    total = pieces[0].astype(jnp.float32)
    for piece in pieces[1:]:
        total = total + piece.astype(jnp.float32)
    return total.astype(jnp.bfloat16)


class Line:
    def __init__(self, name, size, inner):
        self.name, self.size, self.inner = name, size, inner
        self.place = lax.axis_index(name) // inner % size

    def move(self, value, shift, allowed):
        pairs = []
        for source in range(lax.axis_size(self.name)):
            place = source // self.inner % self.size
            if place in allowed and 0 <= place + shift < self.size:
                pairs.append((source, source + shift * self.inner))
        return lax.ppermute(value, self.name, pairs)

    def swap(self, value):
        pairs = []
        for source in range(lax.axis_size(self.name)):
            place = source // self.inner % self.size
            pairs.append((source, source + (1 - 2 * place) * self.inner))
        return lax.ppermute(value, self.name, pairs)

    def scatter(self, parts, axis):
        size = self.size
        if size == 1:
            return pick(parts, axis, 0)
        own = pick(parts, axis, self.place)
        if size == 2:
            return add_low(own, self.swap(pick(parts, axis, 1 - self.place)))
        rising = pick(parts, axis, jnp.minimum(self.place + size - 1, size - 1))
        falling = pick(parts, axis, jnp.maximum(self.place - size + 1, 0))
        for step in range(1, size):
            rising = self.move(rising, 1, range(step))
            falling = self.move(falling, -1, range(size - step, size))
            if step < size - 1:
                up = jnp.minimum(self.place + size - step - 1, size - 1)
                down = jnp.maximum(self.place - size + step + 1, 0)
                rising = add_low(pick(parts, axis, up), rising)
                falling = add_low(pick(parts, axis, down), falling)
        return add_low(own, rising, falling)


def lines():
    rows = lax.axis_size("dp")
    columns = lax.axis_size("fsdp")
    short = 1 << ((columns.bit_length() - 1) // 2)
    return (
        Line("dp", 2, 1),
        Line("dp", rows // 2, 2),
        Line("fsdp", short, 1),
        Line("fsdp", columns // short, short),
    )


class Scatter:
    def __init__(self, terms):
        self.core, self.across, self.up, self.deep = lines()
        self.sizes = [term.shape[1] for term in terms]
        blocks = [
            term.reshape(self.across.size, 2, self.deep.size, self.up.size, -1, term.shape[1])
            for term in terms
        ]
        self.widths = [block.shape[4] for block in blocks]
        self.own = [pick(block, 1, self.core.place) for block in blocks]
        self.sent = [pick(block, 1, 1 - self.core.place) for block in blocks]

    def to_core(self):
        sums = [add_low(own, self.core.swap(sent)) for own, sent in zip(self.own, self.sent)]
        pieces = [piece for total in sums for piece in lane_rows(total)]
        parts = jnp.concatenate(pieces, axis=-2)
        self.left, self.right = parts[..., : D // 2], parts[..., D // 2 :]

    def to_first(self):
        self.left = self.across.scatter(self.left, 0)
        self.right = self.up.scatter(self.right, 2)

    def to_second(self):
        self.left = self.up.scatter(self.left, 1)
        self.right = self.across.scatter(self.right, 0)
        self.left = jnp.concatenate([self.left, self.right], axis=-1)

    def to_owner(self):
        summed = self.deep.scatter(self.left, 0).astype(jnp.float32)
        outs, start = [], 0
        for size, width in zip(self.sizes, self.widths):
            count = -(-size // D)
            columns = [
                summed[start + index * width : start + (index + 1) * width]
                for index in range(count)
            ]
            joined = columns[0] if count == 1 else jnp.concatenate(columns, axis=1)[:, :size]
            outs.append(jnp.transpose(joined))
            start += count * width
        return outs


def weight_term(left, right):
    return weight_dot(left, right).astype(jnp.bfloat16)


def per_device(
    inputs,
    lengths,
    query_weight,
    key_weight,
    value_weight,
    gate_weight,
    out_weight,
    first_weight,
    second_weight,
    down_weight,
    cotangent,
):
    shards = lax.axis_size(AXES)
    query_t, key_t, value_t, gate_t, out_t = gather_rows(
        (query_weight, key_weight, value_weight, gate_weight, out_weight), shards
    )
    first_t, second_t, down_t = gather_rows((first_weight, second_weight, down_weight), shards)
    inputs_f = inputs.astype(jnp.float32)
    length = inputs.shape[0]
    mask = (lax.iota(jnp.int32, length) < lengths[0]).astype(jnp.float32)[:, None]
    tables = make_tables(length)
    normed = simple_norm(inputs_f).astype(jnp.bfloat16)
    query_pre = back_dot(normed, query_t)
    key_pre = back_dot(normed, key_t)
    value_pre = back_dot(normed, value_t)
    gate_pre = back_dot(normed, gate_t)
    attended = lightning_forward(lengths, query_pre, key_pre, value_pre, tables)
    attended_norm = simple_norm(attended)
    gated = (attended_norm * gate_pre * mask).astype(jnp.bfloat16)
    mixed = inputs_f + back_dot(gated, out_t)
    normed_two = simple_norm(mixed).astype(jnp.bfloat16)
    first = back_dot(normed_two, first_t)
    second = back_dot(normed_two, second_t)
    product_low = (first * second * mask).astype(jnp.bfloat16)
    result = mixed + back_dot(product_low, down_t)
    product_grad = forward_dot(cotangent, down_t)
    first_low = (product_grad * second * mask).astype(jnp.bfloat16)
    second_low = (product_grad * first * mask).astype(jnp.bfloat16)
    normed_two_grad = forward_dot(first_low, first_t) + forward_dot(second_low, second_t)
    glu = Scatter(
        [
            weight_term(first_low, normed_two),
            weight_term(second_low, normed_two),
            weight_term(cotangent, product_low),
        ]
    )
    mixed_grad = cotangent.astype(jnp.float32) + norm_back(mixed, normed_two_grad)
    mixed_low = mixed_grad.astype(jnp.bfloat16)
    mixed_low, glu.sent = lax.optimization_barrier((mixed_low, glu.sent))
    glu.to_core()
    gated_grad = forward_dot(mixed_low, out_t)
    gate_low = (gated_grad * attended_norm * mask).astype(jnp.bfloat16)
    attended_low = norm_back(attended, gated_grad * gate_pre * mask).astype(jnp.bfloat16)
    attended_low, glu.left, glu.right = lax.optimization_barrier(
        (attended_low, glu.left, glu.right)
    )
    glu.to_first()
    query_low, key_low, value_low = lightning_backward(
        lengths, query_pre, key_pre, value_pre, attended_low, tables
    )
    query_low, key_low, value_low, glu.left, glu.right = lax.optimization_barrier(
        (query_low, key_low, value_low, glu.left, glu.right)
    )
    late = Scatter(
        [
            weight_term(mixed_low, gated),
            weight_term(gate_low, normed),
            weight_term(query_low, normed),
            weight_term(key_low, normed),
            weight_term(value_low, normed),
        ]
    )
    glu.to_second()
    late.sent, glu.left = lax.optimization_barrier((late.sent, glu.left))
    late.to_core()
    first_sum, second_sum, down_sum = glu.to_owner()
    normed_grad = (
        forward_dot(query_low, query_t)
        + forward_dot(key_low, key_t)
        + forward_dot(value_low, value_t)
        + forward_dot(gate_low, gate_t)
    )
    input_grad = mixed_grad + norm_back(inputs_f, normed_grad)
    late.to_first()
    late.to_second()
    out_sum, gate_sum, query_sum, key_sum, value_sum = late.to_owner()
    return (
        result.astype(jnp.bfloat16),
        input_grad,
        query_sum,
        key_sum,
        value_sum,
        gate_sum,
        out_sum,
        first_sum,
        second_sum,
        down_sum,
    )


def solution(mesh):
    return jax.shard_map(
        per_device,
        mesh=mesh,
        in_specs=(
            P(("dp", "fsdp"), None),
            P(("dp", "fsdp")),
            P(None, ("dp", "fsdp")),
            P(None, ("dp", "fsdp")),
            P(None, ("dp", "fsdp")),
            P(None, ("dp", "fsdp")),
            P(None, ("dp", "fsdp")),
            P(None, ("dp", "fsdp")),
            P(None, ("dp", "fsdp")),
            P(None, ("dp", "fsdp")),
            P(("dp", "fsdp"), None),
        ),
        out_specs=(
            P(("dp", "fsdp"), None),
            P(("dp", "fsdp"), None),
            P(None, ("dp", "fsdp")),
            P(None, ("dp", "fsdp")),
            P(None, ("dp", "fsdp")),
            P(None, ("dp", "fsdp")),
            P(None, ("dp", "fsdp")),
            P(None, ("dp", "fsdp")),
            P(None, ("dp", "fsdp")),
            P(None, ("dp", "fsdp")),
        ),
        check_vma=False,
    )
```

```python
import math

import jax
import jax.numpy as jnp
from jax import lax
from jax.experimental import pallas as pl
from jax.experimental.pallas import tpu as pltpu
from jax.sharding import PartitionSpec as P

D = 1024
HEADS = 8
HEAD = 128
SPAN = 256
LAYER = 12
LAYERS = 24


NORM_EPS = 1e-06


def simple_norm(values):
    return values * lax.rsqrt(jnp.mean(values * values, axis=-1, keepdims=True) + NORM_EPS)


def norm_back(values, upstream):
    return jax.vjp(simple_norm, values)[1](upstream)[0]


def forward_dot(left, right):
    return jnp.dot(left, right, preferred_element_type=jnp.float32)


def back_dot(left, right):
    return lax.dot_general(
        left, right, (((1,), (1,)), ((), ())), preferred_element_type=jnp.float32
    )


def weight_dot(left, right):
    return lax.dot_general(
        left, right, (((0,), (0,)), ((), ())), preferred_element_type=jnp.float32
    )


def make_tables(length):
    head_index = jnp.arange(HEADS, dtype=jnp.float32)
    slopes = jnp.exp2(-8.0 * (head_index + 1.0) / HEADS) * (1.0 - LAYER / LAYERS)
    places = jnp.arange(length, dtype=jnp.float32)
    frequency = jnp.exp(-jnp.arange(HEAD, dtype=jnp.float32) * (math.log(10000.0) / HEAD))
    angles = places[:, None] * frequency[None, :]
    return (jnp.cos(angles), jnp.sin(angles), slopes)


def dot_nn(left, right):
    return lax.dot_general(
        left, right, (((1,), (0,)), ((), ())), preferred_element_type=jnp.float32
    )


def decays(slope):
    rows = lax.broadcasted_iota(jnp.int32, (SPAN, SPAN), 0).astype(jnp.float32)
    columns = lax.broadcasted_iota(jnp.int32, (SPAN, SPAN), 1).astype(jnp.float32)
    distance = rows - columns
    within = jnp.where(distance >= 0.0, jnp.exp(-slope * jnp.maximum(distance, 0.0)), 0.0)
    query_decay = jnp.exp(-(rows + 1.0) * slope)
    key_decay = jnp.exp(-(SPAN - 1.0 - rows) * slope)
    block_decay = jnp.exp(jnp.full((1, HEAD), -SPAN, jnp.float32) * slope)
    return within, query_decay, key_decay, block_decay


def span_rows(block):
    return pl.ds(block * SPAN, SPAN)


def span_mask(block, count):
    places = lax.broadcasted_iota(jnp.int32, (SPAN, HEAD), 0) + block * SPAN
    return (places < count).astype(jnp.float32)


def turned(pre, mask, cosine, sine):
    active = pre * jax.nn.sigmoid(pre) * mask
    return jnp.concatenate([active * cosine, active * sine], axis=-1).astype(jnp.bfloat16)


def scaled(turned_block, decay):
    return (turned_block.astype(jnp.float32) * decay).astype(jnp.bfloat16)


def forward_kernel(count_ref, slope_ref, query_ref, key_ref, value_ref, cosine_ref, sine_ref, out_ref):
    within, query_decay, key_decay, block_decay = decays(slope_ref[pl.program_id(0)])
    state = jnp.zeros((2 * HEAD, HEAD), jnp.float32)
    for block in range(query_ref.shape[0] // SPAN):
        rows = span_rows(block)
        mask = span_mask(block, count_ref[0])
        cosine, sine = cosine_ref[rows, :], sine_ref[rows, :]
        query = turned(query_ref[rows, :], mask, cosine, sine)
        key = turned(key_ref[rows, :], mask, cosine, sine)
        value = (value_ref[rows, :] * mask).astype(jnp.bfloat16)
        weights_low = (back_dot(query, key) * within).astype(jnp.bfloat16)
        out_ref[rows, :] = dot_nn(weights_low, value) + dot_nn(
            scaled(query, query_decay), state.astype(jnp.bfloat16)
        )
        state = block_decay * state + weight_dot(scaled(key, key_decay), value)


def silu_slope(pre):
    gate = jax.nn.sigmoid(pre)
    return gate * (1.0 + pre * (1.0 - gate))


def backward_kernel(
    count_ref,
    slope_ref,
    query_ref,
    key_ref,
    value_ref,
    upstream_ref,
    cosine_ref,
    sine_ref,
    query_low_ref,
    key_low_ref,
    value_low_ref,
    state_ref,
):
    within, query_decay, key_decay, block_decay = decays(slope_ref[pl.program_id(0)])
    blocks = query_ref.shape[0] // SPAN
    state = jnp.zeros((2 * HEAD, HEAD), jnp.float32)
    for block in range(blocks):
        state_ref[block] = state.astype(jnp.bfloat16)
        if block + 1 < blocks:
            rows = span_rows(block)
            mask = span_mask(block, count_ref[0])
            key = turned(key_ref[rows, :], mask, cosine_ref[rows, :], sine_ref[rows, :])
            value = (value_ref[rows, :] * mask).astype(jnp.bfloat16)
            state = block_decay * state + weight_dot(scaled(key, key_decay), value)
    later = jnp.zeros((2 * HEAD, HEAD), jnp.bfloat16)
    for block in reversed(range(blocks)):
        rows = span_rows(block)
        mask = span_mask(block, count_ref[0])
        cosine, sine = cosine_ref[rows, :], sine_ref[rows, :]
        query_pre, key_pre = query_ref[rows, :], key_ref[rows, :]
        query = turned(query_pre, mask, cosine, sine)
        key = turned(key_pre, mask, cosine, sine)
        value = (value_ref[rows, :] * mask).astype(jnp.bfloat16)
        upstream = upstream_ref[rows, :]
        weights_low = (back_dot(query, key) * within).astype(jnp.bfloat16)
        score_low = (back_dot(upstream, value) * within).astype(jnp.bfloat16)
        query_grad = dot_nn(score_low, key) + query_decay * back_dot(upstream, state_ref[block])
        key_grad = weight_dot(score_low, query) + key_decay * back_dot(value, later)
        value_grad = weight_dot(weights_low, upstream) + dot_nn(scaled(key, key_decay), later)
        query_back = (query_grad[:, :HEAD] * cosine + query_grad[:, HEAD:] * sine) * mask
        key_back = (key_grad[:, :HEAD] * cosine + key_grad[:, HEAD:] * sine) * mask
        query_low_ref[rows, :] = (silu_slope(query_pre) * query_back).astype(jnp.bfloat16)
        key_low_ref[rows, :] = (silu_slope(key_pre) * key_back).astype(jnp.bfloat16)
        value_low_ref[rows, :] = (value_grad * mask).astype(jnp.bfloat16)
        if block > 0:
            term = weight_dot(scaled(query, query_decay), upstream)
            later = (block_decay * later.astype(jnp.float32) + term).astype(jnp.bfloat16)


def head_specs(length, count):
    return [pl.BlockSpec((length, HEAD), lambda head: (0, head)) for _ in range(count)]


def shared_specs(length):
    return [pl.BlockSpec((length, HEAD), lambda head: (0, 0)) for _ in range(2)]


def scalar_specs():
    return [pl.BlockSpec(memory_space=pltpu.SMEM) for _ in range(2)]


def lightning_forward(lengths, query_pre, key_pre, value_pre, tables, interpret=False):
    length = query_pre.shape[0]
    return pl.pallas_call(
        forward_kernel,
        grid=(HEADS,),
        in_specs=scalar_specs() + head_specs(length, 3) + shared_specs(length),
        out_specs=head_specs(length, 1)[0],
        out_shape=jax.ShapeDtypeStruct((length, D), jnp.float32),
        name="lightning_forward",
        interpret=interpret,
    )(lengths, tables[2], query_pre, key_pre, value_pre, tables[0], tables[1])


def lightning_backward(lengths, query_pre, key_pre, value_pre, upstream, tables, interpret=False):
    length = query_pre.shape[0]
    return pl.pallas_call(
        backward_kernel,
        grid=(HEADS,),
        in_specs=scalar_specs() + head_specs(length, 4) + shared_specs(length),
        out_specs=head_specs(length, 3),
        out_shape=[jax.ShapeDtypeStruct((length, D), jnp.bfloat16)] * 3,
        scratch_shapes=[pltpu.VMEM((length // SPAN, 2 * HEAD, HEAD), jnp.bfloat16)],
        name="lightning_backward",
        interpret=interpret,
    )(lengths, tables[2], query_pre, key_pre, value_pre, upstream, tables[0], tables[1])


AXES = ("dp", "fsdp")


def lane_rows(matrix):
    extra = -matrix.shape[-1] % D
    if extra:
        matrix = jnp.pad(matrix, [(0, 0)] * (matrix.ndim - 1) + [(0, extra)])
    return jnp.split(matrix, matrix.shape[-1] // D, axis=-1)


def pick(parts, axis, index):
    return lax.dynamic_index_in_dim(parts, index, axis, keepdims=False)


def add_low(*pieces):
    total = pieces[0].astype(jnp.float32)
    for piece in pieces[1:]:
        total = total + piece.astype(jnp.float32)
    return total.astype(jnp.bfloat16)


class Line:
    def __init__(self, name, size, inner):
        self.name, self.size, self.inner = name, size, inner
        self.place = lax.axis_index(name) // inner % size

    def move(self, value, shift, allowed):
        pairs = []
        for source in range(lax.axis_size(self.name)):
            place = source // self.inner % self.size
            if place in allowed and 0 <= place + shift < self.size:
                pairs.append((source, source + shift * self.inner))
        return lax.ppermute(value, self.name, pairs)

    def swap(self, value):
        pairs = []
        for source in range(lax.axis_size(self.name)):
            place = source // self.inner % self.size
            pairs.append((source, source + (1 - 2 * place) * self.inner))
        return lax.ppermute(value, self.name, pairs)

    def scatter(self, parts, axis):
        size = self.size
        if size == 1:
            return pick(parts, axis, 0)
        own = pick(parts, axis, self.place)
        if size == 2:
            return add_low(own, self.swap(pick(parts, axis, 1 - self.place)))
        rising = pick(parts, axis, jnp.minimum(self.place + size - 1, size - 1))
        falling = pick(parts, axis, jnp.maximum(self.place - size + 1, 0))
        for step in range(1, size):
            rising = self.move(rising, 1, range(step))
            falling = self.move(falling, -1, range(size - step, size))
            if step < size - 1:
                up = jnp.minimum(self.place + size - step - 1, size - 1)
                down = jnp.maximum(self.place - size + step + 1, 0)
                rising = add_low(pick(parts, axis, up), rising)
                falling = add_low(pick(parts, axis, down), falling)
        return add_low(own, rising, falling)


    def paired(self, own, other, axis):
        low = jnp.stack([own, other], axis=axis)
        high = jnp.stack([other, own], axis=axis)
        return jnp.where(self.place == 0, low, high)

    def gather(self, shard, axis):
        size = self.size
        if size == 1:
            return jnp.expand_dims(shard, axis)
        if size == 2:
            return self.paired(shard, self.swap(shard), axis)
        rising, falling = [shard], [shard]
        for step in range(1, size):
            rising.append(self.move(rising[-1], 1, range(step - 1, size)))
            falling.append(self.move(falling[-1], -1, range(size - step + 1)))
        known = jnp.stack(rising[:0:-1] + falling, axis=axis)
        return lax.dynamic_slice_in_dim(known, size - 1 - self.place, size, axis)


def lines():
    rows = lax.axis_size("dp")
    columns = lax.axis_size("fsdp")
    short = 1 << ((columns.bit_length() - 1) // 2)
    return (
        Line("dp", 2, 1),
        Line("dp", rows // 2, 2),
        Line("fsdp", short, 1),
        Line("fsdp", columns // short, short),
    )


def packed(matrices):
    return jnp.concatenate(
        [piece for matrix in matrices for piece in lane_rows(jnp.transpose(matrix))], axis=0
    )


def unpacked(full, matrices, shards):
    gathered, start = [], 0
    for matrix in matrices:
        size, width = matrix.shape
        count = -(-size // D)
        columns = [
            full(start + index * width, start + (index + 1) * width).reshape(shards * width, D)
            for index in range(count)
        ]
        joined = columns[0] if count == 1 else jnp.concatenate(columns, axis=1)[:, :size]
        gathered.append(joined)
        start += count * width
    return gathered


def gather_rows(matrices, shards):
    full = lax.all_gather(packed(matrices), AXES, axis=0, tiled=True)
    full = full.reshape(shards, -1, D)
    return unpacked(lambda start, stop: full[:, start:stop], matrices, shards)


def gather_stages(matrices, shards):
    core, across, up, deep = lines()
    shard = deep.gather(packed(matrices), 0)
    left = up.gather(across.gather(shard[..., : D // 2], 0), 2)
    right = across.gather(up.gather(shard[..., D // 2 :], 1), 0)
    halves = [(half, core.swap(half)) for half in (left, right)]

    def rows(start, stop):
        pieces = [
            core.paired(own[..., start:stop, :], other[..., start:stop, :], 1)
            for own, other in halves
        ]
        return jnp.concatenate(pieces, axis=-1)

    return unpacked(rows, matrices, shards)


class Scatter:
    def __init__(self, terms):
        self.core, self.across, self.up, self.deep = lines()
        self.sizes = [term.shape[1] for term in terms]
        blocks = [
            term.reshape(self.across.size, 2, self.deep.size, self.up.size, -1, term.shape[1])
            for term in terms
        ]
        self.widths = [block.shape[4] for block in blocks]
        self.own = [pick(block, 1, self.core.place) for block in blocks]
        self.sent = [pick(block, 1, 1 - self.core.place) for block in blocks]

    def to_core(self):
        sums = [add_low(own, self.core.swap(sent)) for own, sent in zip(self.own, self.sent)]
        pieces = [piece for total in sums for piece in lane_rows(total)]
        parts = jnp.concatenate(pieces, axis=-2)
        self.left, self.right = parts[..., : D // 2], parts[..., D // 2 :]

    def to_first(self):
        self.left = self.across.scatter(self.left, 0)
        self.right = self.up.scatter(self.right, 2)

    def to_second(self):
        self.left = self.up.scatter(self.left, 1)
        self.right = self.across.scatter(self.right, 0)
        self.left = jnp.concatenate([self.left, self.right], axis=-1)

    def to_owner(self):
        self.left = self.deep.scatter(self.left, 0)

    def sums(self):
        summed = self.left.astype(jnp.float32)
        outs, start = [], 0
        for size, width in zip(self.sizes, self.widths):
            count = -(-size // D)
            columns = [
                summed[start + index * width : start + (index + 1) * width]
                for index in range(count)
            ]
            joined = columns[0] if count == 1 else jnp.concatenate(columns, axis=1)[:, :size]
            outs.append(jnp.transpose(joined))
            start += count * width
        return outs


def tie(values):
    return lax.optimization_barrier(values)


def weight_term(left, right):
    return weight_dot(left, right).astype(jnp.bfloat16)


def per_device(
    inputs,
    lengths,
    query_weight,
    key_weight,
    value_weight,
    gate_weight,
    out_weight,
    first_weight,
    second_weight,
    down_weight,
    cotangent,
):
    shards = lax.axis_size(AXES)
    query_t, key_t, value_t, gate_t, out_t = gather_rows(
        (query_weight, key_weight, value_weight, gate_weight, out_weight), shards
    )
    first_t, second_t = gather_stages((first_weight, second_weight), shards)
    (down_t,) = gather_stages((down_weight,), shards)
    inputs_f = inputs.astype(jnp.float32)
    length = inputs.shape[0]
    mask = (lax.iota(jnp.int32, length) < lengths[0]).astype(jnp.float32)[:, None]
    tables = make_tables(length)
    normed = simple_norm(inputs_f).astype(jnp.bfloat16)
    query_pre = back_dot(normed, query_t)
    key_pre = back_dot(normed, key_t)
    value_pre = back_dot(normed, value_t)
    gate_pre = back_dot(normed, gate_t)
    attended = lightning_forward(lengths, query_pre, key_pre, value_pre, tables)
    attended_norm = simple_norm(attended)
    gated = (attended_norm * gate_pre * mask).astype(jnp.bfloat16)
    mixed = inputs_f + back_dot(gated, out_t)
    normed_two = simple_norm(mixed).astype(jnp.bfloat16)
    first = back_dot(normed_two, first_t)
    second = back_dot(normed_two, second_t)
    product_low = (first * second * mask).astype(jnp.bfloat16)
    down = Scatter([weight_term(cotangent, product_low)])
    upstream, product_low, down.sent = tie((cotangent, product_low, down.sent))
    product_grad = forward_dot(upstream, down_t)
    first_low = (product_grad * second * mask).astype(jnp.bfloat16)
    second_low = (product_grad * first * mask).astype(jnp.bfloat16)
    down.to_core()
    first_low, second_low, down.left, down.right = tie(
        (first_low, second_low, down.left, down.right)
    )
    pair = Scatter([weight_term(first_low, normed_two), weight_term(second_low, normed_two)])
    first_low, second_low, pair.sent = tie((first_low, second_low, pair.sent))
    normed_two_grad = forward_dot(first_low, first_t) + forward_dot(second_low, second_t)
    pair.to_core()
    down.to_first()
    normed_two_grad, pair.left, pair.right, down.left, down.right = tie(
        (normed_two_grad, pair.left, pair.right, down.left, down.right)
    )
    mixed_grad = cotangent.astype(jnp.float32) + norm_back(mixed, normed_two_grad)
    mixed_low = mixed_grad.astype(jnp.bfloat16)
    gated_grad = forward_dot(mixed_low, out_t)
    gate_low = (gated_grad * attended_norm * mask).astype(jnp.bfloat16)
    attended_low = norm_back(attended, gated_grad * gate_pre * mask).astype(jnp.bfloat16)
    early = Scatter([weight_term(mixed_low, gated), weight_term(gate_low, normed)])
    down.to_second()
    attended_low, early.sent, down.left = tie((attended_low, early.sent, down.left))
    query_low, key_low, value_low = lightning_backward(
        lengths, query_pre, key_pre, value_pre, attended_low, tables
    )
    early.to_core()
    pair.to_first()
    query_low, key_low, value_low, early.left, early.right, pair.left, pair.right = tie(
        (query_low, key_low, value_low, early.left, early.right, pair.left, pair.right)
    )
    late = Scatter(
        [
            weight_term(query_low, normed),
            weight_term(key_low, normed),
            weight_term(value_low, normed),
        ]
    )
    down.to_owner()
    pair.to_second()
    query_low, key_low, value_low, gate_low, product_low, late.sent, pair.left, down.left = tie(
        (query_low, key_low, value_low, gate_low, product_low, late.sent, pair.left, down.left)
    )
    late.to_core()
    early.to_first()
    result = mixed + back_dot(product_low, down_t)
    result, early.left, early.right = tie((result, early.left, early.right))
    normed_grad = (
        forward_dot(query_low, query_t)
        + forward_dot(key_low, key_t)
        + forward_dot(value_low, value_t)
        + forward_dot(gate_low, gate_t)
    )
    input_grad = mixed_grad + norm_back(inputs_f, normed_grad)
    late.to_first()
    early.to_second()
    pair.to_owner()
    late.to_second()
    early.to_owner()
    late.to_owner()
    (down_sum,) = down.sums()
    first_sum, second_sum = pair.sums()
    out_sum, gate_sum = early.sums()
    query_sum, key_sum, value_sum = late.sums()
    return (
        result.astype(jnp.bfloat16),
        input_grad,
        query_sum,
        key_sum,
        value_sum,
        gate_sum,
        out_sum,
        first_sum,
        second_sum,
        down_sum,
    )


def solution(mesh):
    return jax.shard_map(
        per_device,
        mesh=mesh,
        in_specs=(
            P(("dp", "fsdp"), None),
            P(("dp", "fsdp")),
            P(None, ("dp", "fsdp")),
            P(None, ("dp", "fsdp")),
            P(None, ("dp", "fsdp")),
            P(None, ("dp", "fsdp")),
            P(None, ("dp", "fsdp")),
            P(None, ("dp", "fsdp")),
            P(None, ("dp", "fsdp")),
            P(None, ("dp", "fsdp")),
            P(("dp", "fsdp"), None),
        ),
        out_specs=(
            P(("dp", "fsdp"), None),
            P(("dp", "fsdp"), None),
            P(None, ("dp", "fsdp")),
            P(None, ("dp", "fsdp")),
            P(None, ("dp", "fsdp")),
            P(None, ("dp", "fsdp")),
            P(None, ("dp", "fsdp")),
            P(None, ("dp", "fsdp")),
            P(None, ("dp", "fsdp")),
            P(None, ("dp", "fsdp")),
        ),
        check_vma=False,
    )
```

```python
import math

import jax
import jax.numpy as jnp
from jax import lax
from jax.experimental import pallas as pl
from jax.experimental.pallas import tpu as pltpu
from jax.sharding import PartitionSpec as P

D = 1024
HEADS = 8
HEAD = 128
SPAN = 256
LAYER = 12
LAYERS = 24


NORM_EPS = 1e-06


def simple_norm(values):
    return values * lax.rsqrt(jnp.mean(values * values, axis=-1, keepdims=True) + NORM_EPS)


def norm_back(values, upstream):
    return jax.vjp(simple_norm, values)[1](upstream)[0]


def forward_dot(left, right):
    return jnp.dot(left, right, preferred_element_type=jnp.float32)


def back_dot(left, right):
    return lax.dot_general(
        left, right, (((1,), (1,)), ((), ())), preferred_element_type=jnp.float32
    )


def weight_dot(left, right):
    return lax.dot_general(
        left, right, (((0,), (0,)), ((), ())), preferred_element_type=jnp.float32
    )


def make_tables(length):
    head_index = jnp.arange(HEADS, dtype=jnp.float32)
    slopes = jnp.exp2(-8.0 * (head_index + 1.0) / HEADS) * (1.0 - LAYER / LAYERS)
    places = jnp.arange(length, dtype=jnp.float32)
    frequency = jnp.exp(-jnp.arange(HEAD, dtype=jnp.float32) * (math.log(10000.0) / HEAD))
    angles = places[:, None] * frequency[None, :]
    return (jnp.cos(angles), jnp.sin(angles), slopes)


def dot_nn(left, right):
    return lax.dot_general(
        left, right, (((1,), (0,)), ((), ())), preferred_element_type=jnp.float32
    )


def decays(slope):
    rows = lax.broadcasted_iota(jnp.int32, (SPAN, SPAN), 0).astype(jnp.float32)
    columns = lax.broadcasted_iota(jnp.int32, (SPAN, SPAN), 1).astype(jnp.float32)
    distance = rows - columns
    within = jnp.where(distance >= 0.0, jnp.exp(-slope * jnp.maximum(distance, 0.0)), 0.0)
    query_decay = jnp.exp(-(rows + 1.0) * slope)
    key_decay = jnp.exp(-(SPAN - 1.0 - rows) * slope)
    block_decay = jnp.exp(jnp.full((1, HEAD), -SPAN, jnp.float32) * slope)
    return within, query_decay, key_decay, block_decay


def span_rows(block):
    return pl.ds(block * SPAN, SPAN)


def span_mask(block, count):
    places = lax.broadcasted_iota(jnp.int32, (SPAN, HEAD), 0) + block * SPAN
    return (places < count).astype(jnp.float32)


def turned(pre, mask, cosine, sine):
    active = pre * jax.nn.sigmoid(pre) * mask
    return jnp.concatenate([active * cosine, active * sine], axis=-1).astype(jnp.bfloat16)


def scaled(turned_block, decay):
    return (turned_block.astype(jnp.float32) * decay).astype(jnp.bfloat16)


def forward_kernel(count_ref, slope_ref, query_ref, key_ref, value_ref, cosine_ref, sine_ref, out_ref):
    within, query_decay, key_decay, block_decay = decays(slope_ref[pl.program_id(0)])
    state = jnp.zeros((2 * HEAD, HEAD), jnp.float32)
    for block in range(query_ref.shape[0] // SPAN):
        rows = span_rows(block)
        mask = span_mask(block, count_ref[0])
        cosine, sine = cosine_ref[rows, :], sine_ref[rows, :]
        query = turned(query_ref[rows, :], mask, cosine, sine)
        key = turned(key_ref[rows, :], mask, cosine, sine)
        value = (value_ref[rows, :] * mask).astype(jnp.bfloat16)
        weights_low = (back_dot(query, key) * within).astype(jnp.bfloat16)
        out_ref[rows, :] = dot_nn(weights_low, value) + dot_nn(
            scaled(query, query_decay), state.astype(jnp.bfloat16)
        )
        state = block_decay * state + weight_dot(scaled(key, key_decay), value)


def silu_slope(pre):
    gate = jax.nn.sigmoid(pre)
    return gate * (1.0 + pre * (1.0 - gate))


def backward_kernel(
    count_ref,
    slope_ref,
    query_ref,
    key_ref,
    value_ref,
    upstream_ref,
    cosine_ref,
    sine_ref,
    query_low_ref,
    key_low_ref,
    value_low_ref,
    state_ref,
):
    within, query_decay, key_decay, block_decay = decays(slope_ref[pl.program_id(0)])
    blocks = query_ref.shape[0] // SPAN
    state = jnp.zeros((2 * HEAD, HEAD), jnp.float32)
    for block in range(blocks):
        state_ref[block] = state.astype(jnp.bfloat16)
        if block + 1 < blocks:
            rows = span_rows(block)
            mask = span_mask(block, count_ref[0])
            key = turned(key_ref[rows, :], mask, cosine_ref[rows, :], sine_ref[rows, :])
            value = (value_ref[rows, :] * mask).astype(jnp.bfloat16)
            state = block_decay * state + weight_dot(scaled(key, key_decay), value)
    later = jnp.zeros((2 * HEAD, HEAD), jnp.bfloat16)
    for block in reversed(range(blocks)):
        rows = span_rows(block)
        mask = span_mask(block, count_ref[0])
        cosine, sine = cosine_ref[rows, :], sine_ref[rows, :]
        query_pre, key_pre = query_ref[rows, :], key_ref[rows, :]
        query = turned(query_pre, mask, cosine, sine)
        key = turned(key_pre, mask, cosine, sine)
        value = (value_ref[rows, :] * mask).astype(jnp.bfloat16)
        upstream = upstream_ref[rows, :]
        weights_low = (back_dot(query, key) * within).astype(jnp.bfloat16)
        score_low = (back_dot(upstream, value) * within).astype(jnp.bfloat16)
        query_grad = dot_nn(score_low, key) + query_decay * back_dot(upstream, state_ref[block])
        key_grad = weight_dot(score_low, query) + key_decay * back_dot(value, later)
        value_grad = weight_dot(weights_low, upstream) + dot_nn(scaled(key, key_decay), later)
        query_back = (query_grad[:, :HEAD] * cosine + query_grad[:, HEAD:] * sine) * mask
        key_back = (key_grad[:, :HEAD] * cosine + key_grad[:, HEAD:] * sine) * mask
        query_low_ref[rows, :] = (silu_slope(query_pre) * query_back).astype(jnp.bfloat16)
        key_low_ref[rows, :] = (silu_slope(key_pre) * key_back).astype(jnp.bfloat16)
        value_low_ref[rows, :] = (value_grad * mask).astype(jnp.bfloat16)
        if block > 0:
            term = weight_dot(scaled(query, query_decay), upstream)
            later = (block_decay * later.astype(jnp.float32) + term).astype(jnp.bfloat16)


def head_specs(length, count):
    return [pl.BlockSpec((length, HEAD), lambda head: (0, head)) for _ in range(count)]


def shared_specs(length):
    return [pl.BlockSpec((length, HEAD), lambda head: (0, 0)) for _ in range(2)]


def scalar_specs():
    return [pl.BlockSpec(memory_space=pltpu.SMEM) for _ in range(2)]


def lightning_forward(lengths, query_pre, key_pre, value_pre, tables, interpret=False):
    length = query_pre.shape[0]
    return pl.pallas_call(
        forward_kernel,
        grid=(HEADS,),
        in_specs=scalar_specs() + head_specs(length, 3) + shared_specs(length),
        out_specs=head_specs(length, 1)[0],
        out_shape=jax.ShapeDtypeStruct((length, D), jnp.float32),
        name="lightning_forward",
        interpret=interpret,
    )(lengths, tables[2], query_pre, key_pre, value_pre, tables[0], tables[1])


def lightning_backward(lengths, query_pre, key_pre, value_pre, upstream, tables, interpret=False):
    length = query_pre.shape[0]
    return pl.pallas_call(
        backward_kernel,
        grid=(HEADS,),
        in_specs=scalar_specs() + head_specs(length, 4) + shared_specs(length),
        out_specs=head_specs(length, 3),
        out_shape=[jax.ShapeDtypeStruct((length, D), jnp.bfloat16)] * 3,
        scratch_shapes=[pltpu.VMEM((length // SPAN, 2 * HEAD, HEAD), jnp.bfloat16)],
        name="lightning_backward",
        interpret=interpret,
    )(lengths, tables[2], query_pre, key_pre, value_pre, upstream, tables[0], tables[1])


AXES = ("dp", "fsdp")
ROWS = 24


def lane_rows(matrix):
    extra = -matrix.shape[-1] % D
    if extra:
        matrix = jnp.pad(matrix, [(0, 0)] * (matrix.ndim - 1) + [(0, extra)])
    return jnp.split(matrix, matrix.shape[-1] // D, axis=-1)


def pick(parts, axis, index):
    return lax.dynamic_index_in_dim(parts, index, axis, keepdims=False)


def add_low(*pieces):
    total = pieces[0].astype(jnp.float32)
    for piece in pieces[1:]:
        total = total + piece.astype(jnp.float32)
    return total.astype(jnp.bfloat16)


class Bit:
    def __init__(self, name, stride):
        self.name, self.stride = name, stride
        self.place = lax.axis_index(name) // stride % 2

    def swap(self, value):
        members = lax.axis_size(self.name)
        pairs = [(source, source ^ self.stride) for source in range(members)]
        return lax.ppermute(value, self.name, pairs)

    def paired(self, own, other, axis):
        low = jnp.stack([own, other], axis=axis)
        high = jnp.stack([other, own], axis=axis)
        return jnp.where(self.place == 0, low, high)


class Cube:
    def __init__(self):
        rows = lax.axis_size("dp")
        columns = lax.axis_size("fsdp")
        short = 1 << ((columns.bit_length() - 1) // 2)
        strides = [("dp", 1 << digit) for digit in reversed(range(rows.bit_length() - 1))]
        strides += [("fsdp", 1 << digit) for digit in reversed(range(columns.bit_length() - 1))]
        self.bits = [Bit(name, stride) for name, stride in strides]
        labels = {key: index for index, key in enumerate(strides)}
        self.core = labels[("dp", 1)]
        across = [labels[key] for key in reversed(strides) if key[0] == "dp" and key[1] > 1]
        up = [labels[key] for key in reversed(strides) if key[0] == "fsdp" and key[1] < short]
        deep = [labels[("fsdp", short)]]
        self.far = [labels[key] for key in reversed(strides) if key[0] == "fsdp" and key[1] > short]
        self.streams = [across + up + deep, up + deep + across, deep + across + up]
        self.cuts = [0, 3 * D // 8, 6 * D // 8, D]

    def columns(self, value):
        return [value[..., low:high] for low, high in zip(self.cuts, self.cuts[1:])]


def packed(matrices):
    return jnp.concatenate(
        [piece for matrix in matrices for piece in lane_rows(jnp.transpose(matrix))], axis=0
    )


def unpacked(full, matrices, shards):
    gathered, start = [], 0
    for matrix in matrices:
        size, width = matrix.shape
        count = -(-size // D)
        columns = [
            full(start + index * width, start + (index + 1) * width).reshape(shards * width, D)
            for index in range(count)
        ]
        joined = columns[0] if count == 1 else jnp.concatenate(columns, axis=1)[:, :size]
        gathered.append(joined)
        start += count * width
    return gathered


def gather_rows(matrices, shards):
    full = lax.all_gather(packed(matrices), AXES, axis=0, tiled=True)
    full = full.reshape(shards, -1, D)
    return unpacked(lambda start, stop: full[:, start:stop], matrices, shards)


class Gather:
    def __init__(self, matrices):
        self.matrices = matrices
        self.cube = Cube()
        value, self.known = packed(matrices), []
        for label in reversed(self.cube.far):
            value = self.join(value, label, self.known)
            self.known = sorted(self.known + [label])
        self.parts = self.cube.columns(value)
        self.done = 0

    def join(self, value, label, known):
        bit = self.cube.bits[label]
        axis = sum(other < label for other in known)
        return bit.paired(value, bit.swap(value), axis)

    def advance(self, stages):
        for stage in range(self.done, self.done + stages):
            for index, stream in enumerate(self.cube.streams):
                order = stream[::-1]
                known = self.known + order[:stage]
                self.parts[index] = self.join(self.parts[index], order[stage], known)
        self.done += stages

    def finish(self, shards):
        bit = self.cube.bits[self.cube.core]
        axis = self.cube.core
        halves = [(part, bit.swap(part)) for part in self.parts]

        def rows(start, stop):
            pieces = [
                bit.paired(own[..., start:stop, :], other[..., start:stop, :], axis)
                for own, other in halves
            ]
            return jnp.concatenate(pieces, axis=-1)

        return unpacked(rows, self.matrices, shards)


class Scatter:
    def __init__(self, terms):
        self.cube = Cube()
        digits = len(self.cube.bits)
        bit = self.cube.bits[self.cube.core]
        blocks = [term.reshape((2,) * digits + (-1, D)) for term in terms]
        self.own = [pick(block, self.cube.core, bit.place) for block in blocks]
        self.sent = [pick(block, self.cube.core, 1 - bit.place) for block in blocks]

    def meet(self, value, label, left):
        bit = self.cube.bits[label]
        axis = sum(other < label for other in left)
        return add_low(pick(value, axis, bit.place), bit.swap(pick(value, axis, 1 - bit.place)))

    def finish(self):
        bit = self.cube.bits[self.cube.core]
        sums = [add_low(own, bit.swap(sent)) for own, sent in zip(self.own, self.sent)]
        parts = self.cube.columns(jnp.stack(sums, axis=-3))
        for stage in range(len(self.cube.streams[0])):
            for index, stream in enumerate(self.cube.streams):
                left = self.cube.far + stream[stage:]
                parts[index] = self.meet(parts[index], stream[stage], left)
        value = jnp.concatenate(parts, axis=-1)
        for position, label in enumerate(self.cube.far):
            value = self.meet(value, label, self.cube.far[position:])
        return [jnp.transpose(value[index].astype(jnp.float32)) for index in range(len(sums))]


def scatter_call(terms, shards):
    pieces, widths = [], []
    for term in terms:
        size = term.shape[1]
        block = term.reshape(shards, -1, size)
        widths.append((size, block.shape[1]))
        pieces += lane_rows(block)
    rows = sum(piece.shape[1] for piece in pieces)
    if rows % ROWS:
        pieces.append(jnp.zeros((shards, -rows % ROWS, D), pieces[0].dtype))
    return jnp.concatenate(pieces, axis=1).reshape(-1, D), widths


def scatter_sums(stacked, widths):
    summed = lax.psum_scatter(stacked, AXES, scatter_dimension=0, tiled=True)
    summed = summed.astype(jnp.float32)
    outs, start = [], 0
    for size, width in widths:
        count = -(-size // D)
        columns = [
            summed[start + index * width : start + (index + 1) * width] for index in range(count)
        ]
        joined = columns[0] if count == 1 else jnp.concatenate(columns, axis=1)[:, :size]
        outs.append(jnp.transpose(joined))
        start += count * width
    return outs


def tie(values):
    return lax.optimization_barrier(values)


def weight_term(left, right):
    return weight_dot(left, right).astype(jnp.bfloat16)


def per_device(
    inputs,
    lengths,
    query_weight,
    key_weight,
    value_weight,
    gate_weight,
    out_weight,
    first_weight,
    second_weight,
    down_weight,
    cotangent,
):
    shards = lax.axis_size(AXES)
    query_t, key_t, value_t, gate_t, out_t = gather_rows(
        (query_weight, key_weight, value_weight, gate_weight, out_weight), shards
    )
    glu = Gather((first_weight, second_weight, down_weight))
    middle = len(glu.cube.streams[0]) - 1
    glu.advance(middle)
    inputs_f = inputs.astype(jnp.float32)
    length = inputs.shape[0]
    mask = (lax.iota(jnp.int32, length) < lengths[0]).astype(jnp.float32)[:, None]
    tables = make_tables(length)
    normed = simple_norm(inputs_f).astype(jnp.bfloat16)
    normed, glu.parts = tie((normed, glu.parts))
    glu.advance(1)
    query_pre = back_dot(normed, query_t)
    key_pre = back_dot(normed, key_t)
    value_pre = back_dot(normed, value_t)
    gate_pre = back_dot(normed, gate_t)
    attended = lightning_forward(lengths, query_pre, key_pre, value_pre, tables)
    attended, glu.parts = tie((attended, glu.parts))
    attended_norm = simple_norm(attended)
    gated = (attended_norm * gate_pre * mask).astype(jnp.bfloat16)
    mixed = inputs_f + back_dot(gated, out_t)
    first_t, second_t, down_t = glu.finish(shards)
    normed_two = simple_norm(mixed).astype(jnp.bfloat16)
    first = back_dot(normed_two, first_t)
    second = back_dot(normed_two, second_t)
    product_low = (first * second * mask).astype(jnp.bfloat16)
    product_grad = forward_dot(cotangent, down_t)
    first_low = (product_grad * second * mask).astype(jnp.bfloat16)
    second_low = (product_grad * first * mask).astype(jnp.bfloat16)
    stacked, widths = scatter_call(
        [
            weight_term(first_low, normed_two),
            weight_term(second_low, normed_two),
            weight_term(cotangent, product_low),
        ],
        shards,
    )
    first_low, second_low, product_low, stacked = tie(
        (first_low, second_low, product_low, stacked)
    )
    first_sum, second_sum, down_sum = scatter_sums(stacked, widths)
    normed_two_grad = forward_dot(first_low, first_t) + forward_dot(second_low, second_t)
    mixed_grad = cotangent.astype(jnp.float32) + norm_back(mixed, normed_two_grad)
    mixed_low = mixed_grad.astype(jnp.bfloat16)
    gated_grad = forward_dot(mixed_low, out_t)
    gate_low = (gated_grad * attended_norm * mask).astype(jnp.bfloat16)
    attended_low = norm_back(attended, gated_grad * gate_pre * mask).astype(jnp.bfloat16)
    query_low, key_low, value_low = lightning_backward(
        lengths, query_pre, key_pre, value_pre, attended_low, tables
    )
    attention = Scatter(
        [
            weight_term(mixed_low, gated),
            weight_term(gate_low, normed),
            weight_term(query_low, normed),
            weight_term(key_low, normed),
            weight_term(value_low, normed),
        ]
    )
    query_low, key_low, value_low, gate_low, product_low, attention.sent = tie(
        (query_low, key_low, value_low, gate_low, product_low, attention.sent)
    )
    result = mixed + back_dot(product_low, down_t)
    normed_grad = (
        forward_dot(query_low, query_t)
        + forward_dot(key_low, key_t)
        + forward_dot(value_low, value_t)
        + forward_dot(gate_low, gate_t)
    )
    input_grad = mixed_grad + norm_back(inputs_f, normed_grad)
    out_sum, gate_sum, query_sum, key_sum, value_sum = attention.finish()
    return (
        result.astype(jnp.bfloat16),
        input_grad,
        query_sum,
        key_sum,
        value_sum,
        gate_sum,
        out_sum,
        first_sum,
        second_sum,
        down_sum,
    )


def solution(mesh):
    return jax.shard_map(
        per_device,
        mesh=mesh,
        in_specs=(
            P(("dp", "fsdp"), None),
            P(("dp", "fsdp")),
            P(None, ("dp", "fsdp")),
            P(None, ("dp", "fsdp")),
            P(None, ("dp", "fsdp")),
            P(None, ("dp", "fsdp")),
            P(None, ("dp", "fsdp")),
            P(None, ("dp", "fsdp")),
            P(None, ("dp", "fsdp")),
            P(None, ("dp", "fsdp")),
            P(("dp", "fsdp"), None),
        ),
        out_specs=(
            P(("dp", "fsdp"), None),
            P(("dp", "fsdp"), None),
            P(None, ("dp", "fsdp")),
            P(None, ("dp", "fsdp")),
            P(None, ("dp", "fsdp")),
            P(None, ("dp", "fsdp")),
            P(None, ("dp", "fsdp")),
            P(None, ("dp", "fsdp")),
            P(None, ("dp", "fsdp")),
            P(None, ("dp", "fsdp")),
        ),
        check_vma=False,
    )
```

```python
import math

import jax
import jax.numpy as jnp
from jax import lax
from jax.experimental import pallas as pl
from jax.experimental.pallas import tpu as pltpu
from jax.sharding import PartitionSpec as P

D = 1024
HEADS = 8
HEAD = 128
SPAN = 256
LAYER = 12
LAYERS = 24


NORM_EPS = 1e-06


def simple_norm(values):
    return values * lax.rsqrt(jnp.mean(values * values, axis=-1, keepdims=True) + NORM_EPS)


def norm_back(values, upstream):
    return jax.vjp(simple_norm, values)[1](upstream)[0]


def forward_dot(left, right):
    return jnp.dot(left, right, preferred_element_type=jnp.float32)


def back_dot(left, right):
    return lax.dot_general(
        left, right, (((1,), (1,)), ((), ())), preferred_element_type=jnp.float32
    )


def weight_dot(left, right):
    return lax.dot_general(
        left, right, (((0,), (0,)), ((), ())), preferred_element_type=jnp.float32
    )


def make_tables(length):
    head_index = jnp.arange(HEADS, dtype=jnp.float32)
    slopes = jnp.exp2(-8.0 * (head_index + 1.0) / HEADS) * (1.0 - LAYER / LAYERS)
    places = jnp.arange(length, dtype=jnp.float32)
    frequency = jnp.exp(-jnp.arange(HEAD, dtype=jnp.float32) * (math.log(10000.0) / HEAD))
    angles = places[:, None] * frequency[None, :]
    return (jnp.cos(angles), jnp.sin(angles), slopes)


def dot_nn(left, right):
    return lax.dot_general(
        left, right, (((1,), (0,)), ((), ())), preferred_element_type=jnp.float32
    )


def decays(slope):
    rows = lax.broadcasted_iota(jnp.int32, (SPAN, SPAN), 0).astype(jnp.float32)
    columns = lax.broadcasted_iota(jnp.int32, (SPAN, SPAN), 1).astype(jnp.float32)
    distance = rows - columns
    within = jnp.where(distance >= 0.0, jnp.exp(-slope * jnp.maximum(distance, 0.0)), 0.0)
    query_decay = jnp.exp(-(rows + 1.0) * slope)
    key_decay = jnp.exp(-(SPAN - 1.0 - rows) * slope)
    block_decay = jnp.exp(jnp.full((1, HEAD), -SPAN, jnp.float32) * slope)
    return within, query_decay, key_decay, block_decay


def span_rows(block):
    return pl.ds(block * SPAN, SPAN)


def span_mask(block, count):
    places = lax.broadcasted_iota(jnp.int32, (SPAN, HEAD), 0) + block * SPAN
    return (places < count).astype(jnp.float32)


def turned(pre, mask, cosine, sine):
    active = pre * jax.nn.sigmoid(pre) * mask
    return jnp.concatenate([active * cosine, active * sine], axis=-1).astype(jnp.bfloat16)


def scaled(turned_block, decay):
    return (turned_block.astype(jnp.float32) * decay).astype(jnp.bfloat16)


def forward_kernel(count_ref, slope_ref, query_ref, key_ref, value_ref, cosine_ref, sine_ref, out_ref):
    within, query_decay, key_decay, block_decay = decays(slope_ref[pl.program_id(0)])
    state = jnp.zeros((2 * HEAD, HEAD), jnp.float32)
    for block in range(query_ref.shape[0] // SPAN):
        rows = span_rows(block)
        mask = span_mask(block, count_ref[0])
        cosine, sine = cosine_ref[rows, :], sine_ref[rows, :]
        query = turned(query_ref[rows, :], mask, cosine, sine)
        key = turned(key_ref[rows, :], mask, cosine, sine)
        value = (value_ref[rows, :] * mask).astype(jnp.bfloat16)
        weights_low = (back_dot(query, key) * within).astype(jnp.bfloat16)
        out_ref[rows, :] = dot_nn(weights_low, value) + dot_nn(
            scaled(query, query_decay), state.astype(jnp.bfloat16)
        )
        state = block_decay * state + weight_dot(scaled(key, key_decay), value)


def silu_slope(pre):
    gate = jax.nn.sigmoid(pre)
    return gate * (1.0 + pre * (1.0 - gate))


def backward_kernel(
    count_ref,
    slope_ref,
    query_ref,
    key_ref,
    value_ref,
    upstream_ref,
    cosine_ref,
    sine_ref,
    query_low_ref,
    key_low_ref,
    value_low_ref,
    state_ref,
):
    within, query_decay, key_decay, block_decay = decays(slope_ref[pl.program_id(0)])
    blocks = query_ref.shape[0] // SPAN
    state = jnp.zeros((2 * HEAD, HEAD), jnp.float32)
    for block in range(blocks):
        state_ref[block] = state.astype(jnp.bfloat16)
        if block + 1 < blocks:
            rows = span_rows(block)
            mask = span_mask(block, count_ref[0])
            key = turned(key_ref[rows, :], mask, cosine_ref[rows, :], sine_ref[rows, :])
            value = (value_ref[rows, :] * mask).astype(jnp.bfloat16)
            state = block_decay * state + weight_dot(scaled(key, key_decay), value)
    later = jnp.zeros((2 * HEAD, HEAD), jnp.bfloat16)
    for block in reversed(range(blocks)):
        rows = span_rows(block)
        mask = span_mask(block, count_ref[0])
        cosine, sine = cosine_ref[rows, :], sine_ref[rows, :]
        query_pre, key_pre = query_ref[rows, :], key_ref[rows, :]
        query = turned(query_pre, mask, cosine, sine)
        key = turned(key_pre, mask, cosine, sine)
        value = (value_ref[rows, :] * mask).astype(jnp.bfloat16)
        upstream = upstream_ref[rows, :]
        weights_low = (back_dot(query, key) * within).astype(jnp.bfloat16)
        score_low = (back_dot(upstream, value) * within).astype(jnp.bfloat16)
        query_grad = dot_nn(score_low, key) + query_decay * back_dot(upstream, state_ref[block])
        key_grad = weight_dot(score_low, query) + key_decay * back_dot(value, later)
        value_grad = weight_dot(weights_low, upstream) + dot_nn(scaled(key, key_decay), later)
        query_back = (query_grad[:, :HEAD] * cosine + query_grad[:, HEAD:] * sine) * mask
        key_back = (key_grad[:, :HEAD] * cosine + key_grad[:, HEAD:] * sine) * mask
        query_low_ref[rows, :] = (silu_slope(query_pre) * query_back).astype(jnp.bfloat16)
        key_low_ref[rows, :] = (silu_slope(key_pre) * key_back).astype(jnp.bfloat16)
        value_low_ref[rows, :] = (value_grad * mask).astype(jnp.bfloat16)
        if block > 0:
            term = weight_dot(scaled(query, query_decay), upstream)
            later = (block_decay * later.astype(jnp.float32) + term).astype(jnp.bfloat16)


def head_specs(length, count):
    return [pl.BlockSpec((length, HEAD), lambda head: (0, head)) for _ in range(count)]


def shared_specs(length):
    return [pl.BlockSpec((length, HEAD), lambda head: (0, 0)) for _ in range(2)]


def scalar_specs():
    return [pl.BlockSpec(memory_space=pltpu.SMEM) for _ in range(2)]


def lightning_forward(lengths, query_pre, key_pre, value_pre, tables, interpret=False):
    length = query_pre.shape[0]
    return pl.pallas_call(
        forward_kernel,
        grid=(HEADS,),
        in_specs=scalar_specs() + head_specs(length, 3) + shared_specs(length),
        out_specs=head_specs(length, 1)[0],
        out_shape=jax.ShapeDtypeStruct((length, D), jnp.float32),
        name="lightning_forward",
        interpret=interpret,
    )(lengths, tables[2], query_pre, key_pre, value_pre, tables[0], tables[1])


def lightning_backward(lengths, query_pre, key_pre, value_pre, upstream, tables, interpret=False):
    length = query_pre.shape[0]
    return pl.pallas_call(
        backward_kernel,
        grid=(HEADS,),
        in_specs=scalar_specs() + head_specs(length, 4) + shared_specs(length),
        out_specs=head_specs(length, 3),
        out_shape=[jax.ShapeDtypeStruct((length, D), jnp.bfloat16)] * 3,
        scratch_shapes=[pltpu.VMEM((length // SPAN, 2 * HEAD, HEAD), jnp.bfloat16)],
        name="lightning_backward",
        interpret=interpret,
    )(lengths, tables[2], query_pre, key_pre, value_pre, upstream, tables[0], tables[1])


AXES = ("dp", "fsdp")
ROWS = 24


def lane_rows(matrix):
    extra = -matrix.shape[-1] % D
    if extra:
        matrix = jnp.pad(matrix, [(0, 0)] * (matrix.ndim - 1) + [(0, extra)])
    return jnp.split(matrix, matrix.shape[-1] // D, axis=-1)


def pick(parts, axis, index):
    return lax.dynamic_index_in_dim(parts, index, axis, keepdims=False)


def add_low(*pieces):
    total = pieces[0].astype(jnp.float32)
    for piece in pieces[1:]:
        total = total + piece.astype(jnp.float32)
    return total.astype(jnp.bfloat16)


class Bit:
    def __init__(self, name, stride):
        self.name, self.stride = name, stride
        self.place = lax.axis_index(name) // stride % 2

    def swap(self, value):
        members = lax.axis_size(self.name)
        pairs = [(source, source ^ self.stride) for source in range(members)]
        return lax.ppermute(value, self.name, pairs)

    def paired(self, own, other, axis):
        low = jnp.stack([own, other], axis=axis)
        high = jnp.stack([other, own], axis=axis)
        return jnp.where(self.place == 0, low, high)


class Cube:
    def __init__(self):
        rows = lax.axis_size("dp")
        columns = lax.axis_size("fsdp")
        short = 1 << ((columns.bit_length() - 1) // 2)
        strides = [("dp", 1 << digit) for digit in reversed(range(rows.bit_length() - 1))]
        strides += [("fsdp", 1 << digit) for digit in reversed(range(columns.bit_length() - 1))]
        self.bits = [Bit(name, stride) for name, stride in strides]
        labels = {key: index for index, key in enumerate(strides)}
        self.core = labels[("dp", 1)]
        across = [labels[key] for key in reversed(strides) if key[0] == "dp" and key[1] > 1]
        up = [labels[key] for key in reversed(strides) if key[0] == "fsdp" and key[1] < short]
        deep = [labels[("fsdp", short)]]
        self.far = [labels[key] for key in reversed(strides) if key[0] == "fsdp" and key[1] > short]
        self.streams = [across + up + deep, up + deep + across, deep + across + up]
        self.cuts = [0, 3 * D // 8, 6 * D // 8, D]

    def columns(self, value):
        return [value[..., low:high] for low, high in zip(self.cuts, self.cuts[1:])]


def packed(matrices):
    return jnp.concatenate(
        [piece for matrix in matrices for piece in lane_rows(jnp.transpose(matrix))], axis=0
    )


def unpacked(full, matrices, shards):
    gathered, start = [], 0
    for matrix in matrices:
        size, width = matrix.shape
        count = -(-size // D)
        columns = [
            full(start + index * width, start + (index + 1) * width).reshape(shards * width, D)
            for index in range(count)
        ]
        joined = columns[0] if count == 1 else jnp.concatenate(columns, axis=1)[:, :size]
        gathered.append(joined)
        start += count * width
    return gathered


class Gather:
    def __init__(self, matrices):
        self.matrices = matrices
        self.cube = Cube()
        self.value, self.known = packed(matrices), []
        self.done = 0

    def begin(self):
        for label in reversed(self.cube.far):
            self.value = self.join(self.value, label, self.known)
            self.known = sorted(self.known + [label])
        self.parts = self.cube.columns(self.value)

    def join(self, value, label, known):
        bit = self.cube.bits[label]
        axis = sum(other < label for other in known)
        return bit.paired(value, bit.swap(value), axis)

    def advance(self, stages):
        for stage in range(self.done, self.done + stages):
            for index, stream in enumerate(self.cube.streams):
                order = stream[::-1]
                known = self.known + order[:stage]
                self.parts[index] = self.join(self.parts[index], order[stage], known)
        self.done += stages

    def finish(self, shards):
        bit = self.cube.bits[self.cube.core]
        axis = self.cube.core
        halves = [(part, bit.swap(part)) for part in self.parts]

        def rows(start, stop):
            pieces = [
                bit.paired(own[..., start:stop, :], other[..., start:stop, :], axis)
                for own, other in halves
            ]
            return jnp.concatenate(pieces, axis=-1)

        return unpacked(rows, self.matrices, shards)


class Scatter:
    def __init__(self, terms):
        self.cube = Cube()
        digits = len(self.cube.bits)
        bit = self.cube.bits[self.cube.core]
        blocks = [term.reshape((2,) * digits + (-1, D)) for term in terms]
        self.own = [pick(block, self.cube.core, bit.place) for block in blocks]
        self.sent = [pick(block, self.cube.core, 1 - bit.place) for block in blocks]

    def meet(self, value, label, left):
        bit = self.cube.bits[label]
        axis = sum(other < label for other in left)
        return add_low(pick(value, axis, bit.place), bit.swap(pick(value, axis, 1 - bit.place)))

    def finish(self):
        bit = self.cube.bits[self.cube.core]
        sums = [add_low(own, bit.swap(sent)) for own, sent in zip(self.own, self.sent)]
        parts = self.cube.columns(jnp.stack(sums, axis=-3))
        for stage in range(len(self.cube.streams[0])):
            for index, stream in enumerate(self.cube.streams):
                left = self.cube.far + stream[stage:]
                parts[index] = self.meet(parts[index], stream[stage], left)
        value = jnp.concatenate(parts, axis=-1)
        for position, label in enumerate(self.cube.far):
            value = self.meet(value, label, self.cube.far[position:])
        return [jnp.transpose(value[index].astype(jnp.float32)) for index in range(len(sums))]


def scatter_call(terms, shards):
    pieces, widths = [], []
    for term in terms:
        size = term.shape[1]
        block = term.reshape(shards, -1, size)
        widths.append((size, block.shape[1]))
        pieces += lane_rows(block)
    rows = sum(piece.shape[1] for piece in pieces)
    if rows % ROWS:
        pieces.append(jnp.zeros((shards, -rows % ROWS, D), pieces[0].dtype))
    return jnp.concatenate(pieces, axis=1).reshape(-1, D), widths


def scatter_sums(stacked, widths):
    summed = lax.psum_scatter(stacked, AXES, scatter_dimension=0, tiled=True)
    summed = summed.astype(jnp.float32)
    outs, start = [], 0
    for size, width in widths:
        count = -(-size // D)
        columns = [
            summed[start + index * width : start + (index + 1) * width] for index in range(count)
        ]
        joined = columns[0] if count == 1 else jnp.concatenate(columns, axis=1)[:, :size]
        outs.append(jnp.transpose(joined))
        start += count * width
    return outs


def tie(values):
    return lax.optimization_barrier(values)


def weight_term(left, right):
    return weight_dot(left, right).astype(jnp.bfloat16)


def per_device(
    inputs,
    lengths,
    query_weight,
    key_weight,
    value_weight,
    gate_weight,
    out_weight,
    first_weight,
    second_weight,
    down_weight,
    cotangent,
):
    shards = lax.axis_size(AXES)
    heads = Gather((query_weight, key_weight, value_weight, gate_weight, out_weight))
    glu = Gather((first_weight, second_weight, down_weight))
    last = len(glu.cube.streams[0])
    heads.begin()
    heads.parts, glu.value = tie((heads.parts, glu.value))
    glu.begin()
    heads.advance(last - 1)
    heads.parts, glu.parts = tie((heads.parts, glu.parts))
    heads.advance(1)
    glu.advance(last - 2)
    heads.parts, glu.parts = tie((heads.parts, glu.parts))
    glu.advance(1)
    query_t, key_t, value_t, gate_t, out_t = heads.finish(shards)
    inputs_f = inputs.astype(jnp.float32)
    length = inputs.shape[0]
    mask = (lax.iota(jnp.int32, length) < lengths[0]).astype(jnp.float32)[:, None]
    tables = make_tables(length)
    normed = simple_norm(inputs_f).astype(jnp.bfloat16)
    query_t, glu.parts = tie((query_t, glu.parts))
    glu.advance(1)
    query_pre = back_dot(normed, query_t)
    key_pre = back_dot(normed, key_t)
    value_pre = back_dot(normed, value_t)
    gate_pre = back_dot(normed, gate_t)
    attended = lightning_forward(lengths, query_pre, key_pre, value_pre, tables)
    attended, glu.parts = tie((attended, glu.parts))
    attended_norm = simple_norm(attended)
    gated = (attended_norm * gate_pre * mask).astype(jnp.bfloat16)
    mixed = inputs_f + back_dot(gated, out_t)
    first_t, second_t, down_t = glu.finish(shards)
    normed_two = simple_norm(mixed).astype(jnp.bfloat16)
    first = back_dot(normed_two, first_t).astype(jnp.bfloat16)
    second = back_dot(normed_two, second_t).astype(jnp.bfloat16)
    product_low = (first.astype(jnp.float32) * second * mask).astype(jnp.bfloat16)
    product_grad = forward_dot(cotangent, down_t)
    first_low = (product_grad * second * mask).astype(jnp.bfloat16)
    second_low = (product_grad * first * mask).astype(jnp.bfloat16)
    stacked, widths = scatter_call(
        [
            weight_term(first_low, normed_two),
            weight_term(second_low, normed_two),
            weight_term(cotangent, product_low),
        ],
        shards,
    )
    first_low, second_low, product_low, stacked = tie(
        (first_low, second_low, product_low, stacked)
    )
    first_sum, second_sum, down_sum = scatter_sums(stacked, widths)
    normed_two_grad = forward_dot(first_low, first_t) + forward_dot(second_low, second_t)
    mixed_grad = cotangent.astype(jnp.float32) + norm_back(mixed, normed_two_grad)
    mixed_low = mixed_grad.astype(jnp.bfloat16)
    gated_grad = forward_dot(mixed_low, out_t)
    gate_low = (gated_grad * attended_norm * mask).astype(jnp.bfloat16)
    attended_low = norm_back(attended, gated_grad * gate_pre * mask).astype(jnp.bfloat16)
    query_low, key_low, value_low = lightning_backward(
        lengths, query_pre, key_pre, value_pre, attended_low, tables
    )
    attention = Scatter(
        [
            weight_term(mixed_low, gated),
            weight_term(gate_low, normed),
            weight_term(query_low, normed),
            weight_term(key_low, normed),
            weight_term(value_low, normed),
        ]
    )
    query_low, key_low, value_low, gate_low, product_low, attention.sent = tie(
        (query_low, key_low, value_low, gate_low, product_low, attention.sent)
    )
    result = mixed + back_dot(product_low, down_t)
    normed_grad = (
        forward_dot(query_low, query_t)
        + forward_dot(key_low, key_t)
        + forward_dot(value_low, value_t)
        + forward_dot(gate_low, gate_t)
    )
    input_grad = mixed_grad + norm_back(inputs_f, normed_grad)
    out_sum, gate_sum, query_sum, key_sum, value_sum = attention.finish()
    return (
        result.astype(jnp.bfloat16),
        input_grad,
        query_sum,
        key_sum,
        value_sum,
        gate_sum,
        out_sum,
        first_sum,
        second_sum,
        down_sum,
    )


def solution(mesh):
    return jax.shard_map(
        per_device,
        mesh=mesh,
        in_specs=(
            P(("dp", "fsdp"), None),
            P(("dp", "fsdp")),
            P(None, ("dp", "fsdp")),
            P(None, ("dp", "fsdp")),
            P(None, ("dp", "fsdp")),
            P(None, ("dp", "fsdp")),
            P(None, ("dp", "fsdp")),
            P(None, ("dp", "fsdp")),
            P(None, ("dp", "fsdp")),
            P(None, ("dp", "fsdp")),
            P(("dp", "fsdp"), None),
        ),
        out_specs=(
            P(("dp", "fsdp"), None),
            P(("dp", "fsdp"), None),
            P(None, ("dp", "fsdp")),
            P(None, ("dp", "fsdp")),
            P(None, ("dp", "fsdp")),
            P(None, ("dp", "fsdp")),
            P(None, ("dp", "fsdp")),
            P(None, ("dp", "fsdp")),
            P(None, ("dp", "fsdp")),
            P(None, ("dp", "fsdp")),
        ),
        check_vma=False,
    )
```

```python
import math

import jax
import jax.numpy as jnp
from jax import lax
from jax.experimental import pallas as pl
from jax.experimental.pallas import tpu as pltpu
from jax.sharding import PartitionSpec as P

D = 1024
HEADS = 8
HEAD = 128
SPAN = 256
LAYER = 12
LAYERS = 24


NORM_EPS = 1e-06


def simple_norm(values):
    return values * lax.rsqrt(jnp.mean(values * values, axis=-1, keepdims=True) + NORM_EPS)


def norm_back(values, upstream):
    return jax.vjp(simple_norm, values)[1](upstream)[0]


def forward_dot(left, right):
    return jnp.dot(left, right, preferred_element_type=jnp.float32)


def back_dot(left, right):
    return lax.dot_general(
        left, right, (((1,), (1,)), ((), ())), preferred_element_type=jnp.float32
    )


def weight_dot(left, right):
    return lax.dot_general(
        left, right, (((0,), (0,)), ((), ())), preferred_element_type=jnp.float32
    )


def make_tables(length):
    head_index = jnp.arange(HEADS, dtype=jnp.float32)
    slopes = jnp.exp2(-8.0 * (head_index + 1.0) / HEADS) * (1.0 - LAYER / LAYERS)
    places = jnp.arange(length, dtype=jnp.float32)
    frequency = jnp.exp(-jnp.arange(HEAD, dtype=jnp.float32) * (math.log(10000.0) / HEAD))
    angles = places[:, None] * frequency[None, :]
    return (jnp.cos(angles), jnp.sin(angles), slopes)


def dot_nn(left, right):
    return lax.dot_general(
        left, right, (((1,), (0,)), ((), ())), preferred_element_type=jnp.float32
    )


def decays(slope):
    rows = lax.broadcasted_iota(jnp.int32, (SPAN, SPAN), 0).astype(jnp.float32)
    columns = lax.broadcasted_iota(jnp.int32, (SPAN, SPAN), 1).astype(jnp.float32)
    distance = rows - columns
    within = jnp.where(distance >= 0.0, jnp.exp(-slope * jnp.maximum(distance, 0.0)), 0.0)
    query_decay = jnp.exp(-(rows + 1.0) * slope)
    key_decay = jnp.exp(-(SPAN - 1.0 - rows) * slope)
    block_decay = jnp.exp(jnp.full((1, HEAD), -SPAN, jnp.float32) * slope)
    return within, query_decay, key_decay, block_decay


def span_rows(block):
    return pl.ds(block * SPAN, SPAN)


def span_mask(block, count):
    places = lax.broadcasted_iota(jnp.int32, (SPAN, HEAD), 0) + block * SPAN
    return (places < count).astype(jnp.float32)


def turned(pre, mask, cosine, sine):
    active = pre * jax.nn.sigmoid(pre) * mask
    return jnp.concatenate([active * cosine, active * sine], axis=-1).astype(jnp.bfloat16)


def scaled(turned_block, decay):
    return (turned_block.astype(jnp.float32) * decay).astype(jnp.bfloat16)


def forward_kernel(count_ref, slope_ref, query_ref, key_ref, value_ref, cosine_ref, sine_ref, out_ref):
    within, query_decay, key_decay, block_decay = decays(slope_ref[pl.program_id(0)])
    state = jnp.zeros((2 * HEAD, HEAD), jnp.float32)
    for block in range(query_ref.shape[0] // SPAN):
        rows = span_rows(block)
        mask = span_mask(block, count_ref[0])
        cosine, sine = cosine_ref[rows, :], sine_ref[rows, :]
        query = turned(query_ref[rows, :], mask, cosine, sine)
        key = turned(key_ref[rows, :], mask, cosine, sine)
        value = (value_ref[rows, :] * mask).astype(jnp.bfloat16)
        weights_low = (back_dot(query, key) * within).astype(jnp.bfloat16)
        out_ref[rows, :] = dot_nn(weights_low, value) + dot_nn(
            scaled(query, query_decay), state.astype(jnp.bfloat16)
        )
        state = block_decay * state + weight_dot(scaled(key, key_decay), value)


def silu_slope(pre):
    gate = jax.nn.sigmoid(pre)
    return gate * (1.0 + pre * (1.0 - gate))


def backward_kernel(
    count_ref,
    slope_ref,
    query_ref,
    key_ref,
    value_ref,
    upstream_ref,
    cosine_ref,
    sine_ref,
    query_low_ref,
    key_low_ref,
    value_low_ref,
    state_ref,
):
    within, query_decay, key_decay, block_decay = decays(slope_ref[pl.program_id(0)])
    blocks = query_ref.shape[0] // SPAN
    state = jnp.zeros((2 * HEAD, HEAD), jnp.float32)
    for block in range(blocks):
        state_ref[block] = state.astype(jnp.bfloat16)
        if block + 1 < blocks:
            rows = span_rows(block)
            mask = span_mask(block, count_ref[0])
            key = turned(key_ref[rows, :], mask, cosine_ref[rows, :], sine_ref[rows, :])
            value = (value_ref[rows, :] * mask).astype(jnp.bfloat16)
            state = block_decay * state + weight_dot(scaled(key, key_decay), value)
    later = jnp.zeros((2 * HEAD, HEAD), jnp.bfloat16)
    for block in reversed(range(blocks)):
        rows = span_rows(block)
        mask = span_mask(block, count_ref[0])
        cosine, sine = cosine_ref[rows, :], sine_ref[rows, :]
        query_pre, key_pre = query_ref[rows, :], key_ref[rows, :]
        query = turned(query_pre, mask, cosine, sine)
        key = turned(key_pre, mask, cosine, sine)
        value = (value_ref[rows, :] * mask).astype(jnp.bfloat16)
        upstream = upstream_ref[rows, :]
        weights_low = (back_dot(query, key) * within).astype(jnp.bfloat16)
        score_low = (back_dot(upstream, value) * within).astype(jnp.bfloat16)
        query_grad = dot_nn(score_low, key) + query_decay * back_dot(upstream, state_ref[block])
        key_grad = weight_dot(score_low, query) + key_decay * back_dot(value, later)
        value_grad = weight_dot(weights_low, upstream) + dot_nn(scaled(key, key_decay), later)
        query_back = (query_grad[:, :HEAD] * cosine + query_grad[:, HEAD:] * sine) * mask
        key_back = (key_grad[:, :HEAD] * cosine + key_grad[:, HEAD:] * sine) * mask
        query_low_ref[rows, :] = (silu_slope(query_pre) * query_back).astype(jnp.bfloat16)
        key_low_ref[rows, :] = (silu_slope(key_pre) * key_back).astype(jnp.bfloat16)
        value_low_ref[rows, :] = (value_grad * mask).astype(jnp.bfloat16)
        if block > 0:
            term = weight_dot(scaled(query, query_decay), upstream)
            later = (block_decay * later.astype(jnp.float32) + term).astype(jnp.bfloat16)


def head_specs(length, count):
    return [pl.BlockSpec((length, HEAD), lambda head: (0, head)) for _ in range(count)]


def shared_specs(length):
    return [pl.BlockSpec((length, HEAD), lambda head: (0, 0)) for _ in range(2)]


def scalar_specs():
    return [pl.BlockSpec(memory_space=pltpu.SMEM) for _ in range(2)]


def lightning_forward(lengths, query_pre, key_pre, value_pre, tables, interpret=False):
    length = query_pre.shape[0]
    return pl.pallas_call(
        forward_kernel,
        grid=(HEADS,),
        in_specs=scalar_specs() + head_specs(length, 3) + shared_specs(length),
        out_specs=head_specs(length, 1)[0],
        out_shape=jax.ShapeDtypeStruct((length, D), jnp.float32),
        name="lightning_forward",
        interpret=interpret,
    )(lengths, tables[2], query_pre, key_pre, value_pre, tables[0], tables[1])


def lightning_backward(lengths, query_pre, key_pre, value_pre, upstream, tables, interpret=False):
    length = query_pre.shape[0]
    return pl.pallas_call(
        backward_kernel,
        grid=(HEADS,),
        in_specs=scalar_specs() + head_specs(length, 4) + shared_specs(length),
        out_specs=head_specs(length, 3),
        out_shape=[jax.ShapeDtypeStruct((length, D), jnp.bfloat16)] * 3,
        scratch_shapes=[pltpu.VMEM((length // SPAN, 2 * HEAD, HEAD), jnp.bfloat16)],
        name="lightning_backward",
        interpret=interpret,
    )(lengths, tables[2], query_pre, key_pre, value_pre, upstream, tables[0], tables[1])


AXES = ("dp", "fsdp")
ROWS = 24


def lane_rows(matrix):
    extra = -matrix.shape[-1] % D
    if extra:
        matrix = jnp.pad(matrix, [(0, 0)] * (matrix.ndim - 1) + [(0, extra)])
    return jnp.split(matrix, matrix.shape[-1] // D, axis=-1)


def pick(parts, axis, index):
    return lax.dynamic_index_in_dim(parts, index, axis, keepdims=False)


def add_low(*pieces):
    total = pieces[0].astype(jnp.float32)
    for piece in pieces[1:]:
        total = total + piece.astype(jnp.float32)
    return total.astype(jnp.bfloat16)


class Bit:
    def __init__(self, name, stride):
        self.name, self.stride = name, stride
        self.place = lax.axis_index(name) // stride % 2

    def swap(self, value):
        members = lax.axis_size(self.name)
        pairs = [(source, source ^ self.stride) for source in range(members)]
        return lax.ppermute(value, self.name, pairs)

    def paired(self, own, other, axis):
        low = jnp.stack([own, other], axis=axis)
        high = jnp.stack([other, own], axis=axis)
        return jnp.where(self.place == 0, low, high)


class Cube:
    def __init__(self):
        rows = lax.axis_size("dp")
        columns = lax.axis_size("fsdp")
        short = 1 << ((columns.bit_length() - 1) // 2)
        strides = [("dp", 1 << digit) for digit in reversed(range(rows.bit_length() - 1))]
        strides += [("fsdp", 1 << digit) for digit in reversed(range(columns.bit_length() - 1))]
        self.bits = [Bit(name, stride) for name, stride in strides]
        labels = {key: index for index, key in enumerate(strides)}
        self.core = labels[("dp", 1)]
        across = [labels[key] for key in reversed(strides) if key[0] == "dp" and key[1] > 1]
        up = [labels[key] for key in reversed(strides) if key[0] == "fsdp" and key[1] < short]
        deep = [labels[("fsdp", short)]]
        self.far = [labels[key] for key in reversed(strides) if key[0] == "fsdp" and key[1] > short]
        self.streams = [across + up + deep, up + deep + across, deep + across + up]
        self.cuts = [0, 3 * D // 8, 6 * D // 8, D]

    def columns(self, value):
        return [value[..., low:high] for low, high in zip(self.cuts, self.cuts[1:])]


def packed(matrices):
    return jnp.concatenate(
        [piece for matrix in matrices for piece in lane_rows(jnp.transpose(matrix))], axis=0
    )


def unpacked(full, matrices, shards):
    gathered, start = [], 0
    for matrix in matrices:
        size, width = matrix.shape
        count = -(-size // D)
        columns = [
            full(start + index * width, start + (index + 1) * width).reshape(shards * width, D)
            for index in range(count)
        ]
        joined = columns[0] if count == 1 else jnp.concatenate(columns, axis=1)[:, :size]
        gathered.append(joined)
        start += count * width
    return gathered


class Gather:
    def __init__(self, matrices):
        self.matrices = matrices
        self.cube = Cube()
        self.value, self.known = packed(matrices), []
        self.done = 0

    def begin(self):
        for label in reversed(self.cube.far):
            self.value = self.join(self.value, label, self.known)
            self.known = sorted(self.known + [label])
        self.parts = self.cube.columns(self.value)

    def join(self, value, label, known):
        bit = self.cube.bits[label]
        axis = sum(other < label for other in known)
        return bit.paired(value, bit.swap(value), axis)

    def advance(self, stages):
        for stage in range(self.done, self.done + stages):
            for index, stream in enumerate(self.cube.streams):
                order = stream[::-1]
                known = self.known + order[:stage]
                self.parts[index] = self.join(self.parts[index], order[stage], known)
        self.done += stages

    def finish(self, shards):
        bit = self.cube.bits[self.cube.core]
        axis = self.cube.core
        halves = [(part, bit.swap(part)) for part in self.parts]

        def rows(start, stop):
            pieces = [
                bit.paired(own[..., start:stop, :], other[..., start:stop, :], axis)
                for own, other in halves
            ]
            return jnp.concatenate(pieces, axis=-1)

        return unpacked(rows, self.matrices, shards)


class Scatter:
    def __init__(self, terms, single=False):
        self.cube = Cube()
        bit = self.cube.bits[self.cube.core]
        shape = (2,) * len(self.cube.bits)
        blocks = [term.reshape(shape + (-1, term.shape[-1])) for term in terms]
        self.own = [pick(block, self.cube.core, bit.place) for block in blocks]
        self.sent = [pick(block, self.cube.core, 1 - bit.place) for block in blocks]
        self.streams = self.cube.streams[:1] if single else self.cube.streams
        self.stage = 0

    def to_core(self):
        bit = self.cube.bits[self.cube.core]
        sums = [add_low(own, bit.swap(sent)) for own, sent in zip(self.own, self.sent)]
        value = jnp.stack(sums, axis=-3)
        self.parts = [value] if len(self.streams) == 1 else self.cube.columns(value)

    def halves(self, value, label, left):
        bit = self.cube.bits[label]
        axis = sum(other < label for other in left)
        return pick(value, axis, bit.place), pick(value, axis, 1 - bit.place)

    def send(self):
        self.own, self.sent, self.labels = [], [], []
        far = self.cube.far
        if self.stage == len(self.streams[0]):
            self.parts = [jnp.concatenate(self.parts, axis=-1)]
        for index, part in enumerate(self.parts):
            order = self.streams[index] + far
            left = order[self.stage :] if self.stage >= len(self.streams[0]) else (
                far + self.streams[index][self.stage :]
            )
            own, sent = self.halves(part, order[self.stage], left)
            self.own.append(own)
            self.sent.append(sent)
            self.labels.append(order[self.stage])
        self.stage += 1

    def meet(self):
        bits = self.cube.bits
        self.parts = [
            add_low(own, bits[label].swap(sent))
            for own, sent, label in zip(self.own, self.sent, self.labels)
        ]

    def finish(self):
        while self.stage < len(self.streams[0]) + len(self.cube.far):
            self.send()
            self.meet()
        (value,) = self.parts
        return [jnp.transpose(value[index].astype(jnp.float32)) for index in range(value.shape[0])]


def scatter_call(terms, shards):
    pieces, widths = [], []
    for term in terms:
        size = term.shape[1]
        block = term.reshape(shards, -1, size)
        widths.append((size, block.shape[1]))
        pieces += lane_rows(block)
    rows = sum(piece.shape[1] for piece in pieces)
    if rows % ROWS:
        pieces.append(jnp.zeros((shards, -rows % ROWS, D), pieces[0].dtype))
    return jnp.concatenate(pieces, axis=1).reshape(-1, D), widths


def scatter_sums(stacked, widths):
    summed = lax.psum_scatter(stacked, AXES, scatter_dimension=0, tiled=True)
    summed = summed.astype(jnp.float32)
    outs, start = [], 0
    for size, width in widths:
        count = -(-size // D)
        columns = [
            summed[start + index * width : start + (index + 1) * width] for index in range(count)
        ]
        joined = columns[0] if count == 1 else jnp.concatenate(columns, axis=1)[:, :size]
        outs.append(jnp.transpose(joined))
        start += count * width
    return outs


def tie(values):
    return lax.optimization_barrier(values)


def after(earlier, value):
    return tie((earlier, value))[1]


def weight_term(left, right):
    return weight_dot(left, right).astype(jnp.bfloat16)


def per_device(
    inputs,
    lengths,
    query_weight,
    key_weight,
    value_weight,
    gate_weight,
    out_weight,
    first_weight,
    second_weight,
    down_weight,
    cotangent,
):
    shards = lax.axis_size(AXES)
    heads = Gather((query_weight, key_weight, value_weight, gate_weight, out_weight))
    glu = Gather((first_weight, second_weight, down_weight))
    last = len(glu.cube.streams[0])
    heads.begin()
    glu.value = after(heads.parts, glu.value)
    heads.advance(last - 1)
    glu.begin()
    glu.parts = after(heads.parts, glu.parts)
    heads.advance(1)
    glu.advance(last - 2)
    glu.parts = after(heads.parts, glu.parts)
    query_t, key_t, value_t, gate_t, out_t = heads.finish(shards)
    glu.advance(1)
    inputs_f = inputs.astype(jnp.float32)
    length = inputs.shape[0]
    mask = (lax.iota(jnp.int32, length) < lengths[0]).astype(jnp.float32)[:, None]
    tables = make_tables(length)
    normed = simple_norm(inputs_f).astype(jnp.bfloat16)
    glu.parts = after(query_t, glu.parts)
    glu.advance(1)
    query_pre = back_dot(normed, query_t)
    key_pre = back_dot(normed, key_t)
    value_pre = back_dot(normed, value_t)
    gate_pre = back_dot(normed, gate_t)
    attended = lightning_forward(lengths, query_pre, key_pre, value_pre, tables)
    attended, glu.parts = tie((attended, glu.parts))
    attended_norm = simple_norm(attended)
    gated = (attended_norm * gate_pre * mask).astype(jnp.bfloat16)
    mixed = inputs_f + back_dot(gated, out_t)
    first_t, second_t, down_t = glu.finish(shards)
    normed_two = simple_norm(mixed).astype(jnp.bfloat16)
    first = back_dot(normed_two, first_t).astype(jnp.bfloat16)
    second = back_dot(normed_two, second_t).astype(jnp.bfloat16)
    product_low = (first.astype(jnp.float32) * second * mask).astype(jnp.bfloat16)
    down = Scatter([weight_term(cotangent, product_low)], single=True)
    product_grad = forward_dot(after(down.sent, cotangent), down_t)
    first_low = (product_grad * second * mask).astype(jnp.bfloat16)
    second_low = (product_grad * first * mask).astype(jnp.bfloat16)
    down.to_core()
    down.send()
    first_low, second_low, down.sent = tie((first_low, second_low, down.sent))
    stacked, widths = scatter_call(
        [weight_term(first_low, normed_two), weight_term(second_low, normed_two)], shards
    )
    first_low, second_low, product_low, stacked = tie(
        (first_low, second_low, product_low, stacked)
    )
    first_sum, second_sum = scatter_sums(stacked, widths)
    normed_two_grad = forward_dot(first_low, first_t) + forward_dot(second_low, second_t)
    down.meet()
    down.send()
    normed_two_grad, down.sent = tie((normed_two_grad, down.sent))
    mixed_grad = cotangent.astype(jnp.float32) + norm_back(mixed, normed_two_grad)
    mixed_low = mixed_grad.astype(jnp.bfloat16)
    gated_grad = forward_dot(mixed_low, out_t)
    gate_low = (gated_grad * attended_norm * mask).astype(jnp.bfloat16)
    attended_low = norm_back(attended, gated_grad * gate_pre * mask).astype(jnp.bfloat16)
    down.meet()
    down.send()
    attended_low, down.sent = tie((attended_low, down.sent))
    query_low, key_low, value_low = lightning_backward(
        lengths, query_pre, key_pre, value_pre, attended_low, tables
    )
    attention = Scatter(
        [
            weight_term(mixed_low, gated),
            weight_term(gate_low, normed),
            weight_term(query_low, normed),
            weight_term(key_low, normed),
            weight_term(value_low, normed),
        ]
    )
    down.meet()
    attention.to_core()
    attention.send()
    query_low, key_low, value_low, gate_low, product_low, attention.sent, down.parts = tie(
        (query_low, key_low, value_low, gate_low, product_low, attention.sent, down.parts)
    )
    result = mixed + back_dot(product_low, down_t)
    normed_grad = (
        forward_dot(query_low, query_t)
        + forward_dot(key_low, key_t)
        + forward_dot(value_low, value_t)
        + forward_dot(gate_low, gate_t)
    )
    input_grad = mixed_grad + norm_back(inputs_f, normed_grad)
    attention.meet()
    (down_sum,) = down.finish()
    out_sum, gate_sum, query_sum, key_sum, value_sum = attention.finish()
    return (
        result.astype(jnp.bfloat16),
        input_grad,
        query_sum,
        key_sum,
        value_sum,
        gate_sum,
        out_sum,
        first_sum,
        second_sum,
        down_sum,
    )


def solution(mesh):
    return jax.shard_map(
        per_device,
        mesh=mesh,
        in_specs=(
            P(("dp", "fsdp"), None),
            P(("dp", "fsdp")),
            P(None, ("dp", "fsdp")),
            P(None, ("dp", "fsdp")),
            P(None, ("dp", "fsdp")),
            P(None, ("dp", "fsdp")),
            P(None, ("dp", "fsdp")),
            P(None, ("dp", "fsdp")),
            P(None, ("dp", "fsdp")),
            P(None, ("dp", "fsdp")),
            P(("dp", "fsdp"), None),
        ),
        out_specs=(
            P(("dp", "fsdp"), None),
            P(("dp", "fsdp"), None),
            P(None, ("dp", "fsdp")),
            P(None, ("dp", "fsdp")),
            P(None, ("dp", "fsdp")),
            P(None, ("dp", "fsdp")),
            P(None, ("dp", "fsdp")),
            P(None, ("dp", "fsdp")),
            P(None, ("dp", "fsdp")),
            P(None, ("dp", "fsdp")),
        ),
        check_vma=False,
    )
```

```python
import math

import jax
import jax.numpy as jnp
from jax import lax
from jax.experimental import pallas as pl
from jax.experimental.pallas import tpu as pltpu
from jax.sharding import PartitionSpec as P

D = 1024
HEADS = 8
HEAD = 128
SPAN = 256
LAYER = 12
LAYERS = 24


NORM_EPS = 1e-06


def simple_norm(values):
    return values * lax.rsqrt(jnp.mean(values * values, axis=-1, keepdims=True) + NORM_EPS)


def norm_back(values, upstream):
    return jax.vjp(simple_norm, values)[1](upstream)[0]


def forward_dot(left, right):
    return jnp.dot(left, right, preferred_element_type=jnp.float32)


def back_dot(left, right):
    return lax.dot_general(
        left, right, (((1,), (1,)), ((), ())), preferred_element_type=jnp.float32
    )


def weight_dot(left, right):
    return lax.dot_general(
        left, right, (((0,), (0,)), ((), ())), preferred_element_type=jnp.float32
    )


def make_tables(length):
    head_index = jnp.arange(HEADS, dtype=jnp.float32)
    slopes = jnp.exp2(-8.0 * (head_index + 1.0) / HEADS) * (1.0 - LAYER / LAYERS)
    places = jnp.arange(length, dtype=jnp.float32)
    frequency = jnp.exp(-jnp.arange(HEAD, dtype=jnp.float32) * (math.log(10000.0) / HEAD))
    angles = places[:, None] * frequency[None, :]
    return (jnp.cos(angles), jnp.sin(angles), slopes)


def dot_nn(left, right):
    return lax.dot_general(
        left, right, (((1,), (0,)), ((), ())), preferred_element_type=jnp.float32
    )


def decays(slope):
    rows = lax.broadcasted_iota(jnp.int32, (SPAN, SPAN), 0).astype(jnp.float32)
    columns = lax.broadcasted_iota(jnp.int32, (SPAN, SPAN), 1).astype(jnp.float32)
    distance = rows - columns
    within = jnp.where(distance >= 0.0, jnp.exp(-slope * jnp.maximum(distance, 0.0)), 0.0)
    query_decay = jnp.exp(-(rows + 1.0) * slope)
    key_decay = jnp.exp(-(SPAN - 1.0 - rows) * slope)
    block_decay = jnp.exp(jnp.full((1, HEAD), -SPAN, jnp.float32) * slope)
    return within, query_decay, key_decay, block_decay


def span_rows(block):
    return pl.ds(block * SPAN, SPAN)


def span_mask(block, count):
    places = lax.broadcasted_iota(jnp.int32, (SPAN, HEAD), 0) + block * SPAN
    return (places < count).astype(jnp.float32)


def turned(pre, mask, cosine, sine):
    active = pre * jax.nn.sigmoid(pre) * mask
    return jnp.concatenate([active * cosine, active * sine], axis=-1).astype(jnp.bfloat16)


def scaled(turned_block, decay):
    return (turned_block.astype(jnp.float32) * decay).astype(jnp.bfloat16)


def forward_kernel(count_ref, slope_ref, query_ref, key_ref, value_ref, cosine_ref, sine_ref, out_ref):
    within, query_decay, key_decay, block_decay = decays(slope_ref[pl.program_id(0)])
    state = jnp.zeros((2 * HEAD, HEAD), jnp.float32)
    for block in range(query_ref.shape[0] // SPAN):
        rows = span_rows(block)
        mask = span_mask(block, count_ref[0])
        cosine, sine = cosine_ref[rows, :], sine_ref[rows, :]
        query = turned(query_ref[rows, :], mask, cosine, sine)
        key = turned(key_ref[rows, :], mask, cosine, sine)
        value = (value_ref[rows, :] * mask).astype(jnp.bfloat16)
        weights_low = (back_dot(query, key) * within).astype(jnp.bfloat16)
        out_ref[rows, :] = dot_nn(weights_low, value) + dot_nn(
            scaled(query, query_decay), state.astype(jnp.bfloat16)
        )
        state = block_decay * state + weight_dot(scaled(key, key_decay), value)


def silu_slope(pre):
    gate = jax.nn.sigmoid(pre)
    return gate * (1.0 + pre * (1.0 - gate))


def backward_kernel(
    count_ref,
    slope_ref,
    query_ref,
    key_ref,
    value_ref,
    upstream_ref,
    cosine_ref,
    sine_ref,
    query_low_ref,
    key_low_ref,
    value_low_ref,
    state_ref,
):
    within, query_decay, key_decay, block_decay = decays(slope_ref[pl.program_id(0)])
    blocks = query_ref.shape[0] // SPAN
    state = jnp.zeros((2 * HEAD, HEAD), jnp.float32)
    for block in range(blocks):
        state_ref[block] = state.astype(jnp.bfloat16)
        if block + 1 < blocks:
            rows = span_rows(block)
            mask = span_mask(block, count_ref[0])
            key = turned(key_ref[rows, :], mask, cosine_ref[rows, :], sine_ref[rows, :])
            value = (value_ref[rows, :] * mask).astype(jnp.bfloat16)
            state = block_decay * state + weight_dot(scaled(key, key_decay), value)
    later = jnp.zeros((2 * HEAD, HEAD), jnp.bfloat16)
    for block in reversed(range(blocks)):
        rows = span_rows(block)
        mask = span_mask(block, count_ref[0])
        cosine, sine = cosine_ref[rows, :], sine_ref[rows, :]
        query_pre, key_pre = query_ref[rows, :], key_ref[rows, :]
        query = turned(query_pre, mask, cosine, sine)
        key = turned(key_pre, mask, cosine, sine)
        value = (value_ref[rows, :] * mask).astype(jnp.bfloat16)
        upstream = upstream_ref[rows, :]
        weights_low = (back_dot(query, key) * within).astype(jnp.bfloat16)
        score_low = (back_dot(upstream, value) * within).astype(jnp.bfloat16)
        query_grad = dot_nn(score_low, key) + query_decay * back_dot(upstream, state_ref[block])
        key_grad = weight_dot(score_low, query) + key_decay * back_dot(value, later)
        value_grad = weight_dot(weights_low, upstream) + dot_nn(scaled(key, key_decay), later)
        query_back = (query_grad[:, :HEAD] * cosine + query_grad[:, HEAD:] * sine) * mask
        key_back = (key_grad[:, :HEAD] * cosine + key_grad[:, HEAD:] * sine) * mask
        query_low_ref[rows, :] = (silu_slope(query_pre) * query_back).astype(jnp.bfloat16)
        key_low_ref[rows, :] = (silu_slope(key_pre) * key_back).astype(jnp.bfloat16)
        value_low_ref[rows, :] = (value_grad * mask).astype(jnp.bfloat16)
        if block > 0:
            term = weight_dot(scaled(query, query_decay), upstream)
            later = (block_decay * later.astype(jnp.float32) + term).astype(jnp.bfloat16)


def head_specs(length, count):
    return [pl.BlockSpec((length, HEAD), lambda head: (0, head)) for _ in range(count)]


def shared_specs(length):
    return [pl.BlockSpec((length, HEAD), lambda head: (0, 0)) for _ in range(2)]


def scalar_specs():
    return [pl.BlockSpec(memory_space=pltpu.SMEM) for _ in range(2)]


def lightning_forward(lengths, query_pre, key_pre, value_pre, tables, interpret=False):
    length = query_pre.shape[0]
    return pl.pallas_call(
        forward_kernel,
        grid=(HEADS,),
        in_specs=scalar_specs() + head_specs(length, 3) + shared_specs(length),
        out_specs=head_specs(length, 1)[0],
        out_shape=jax.ShapeDtypeStruct((length, D), jnp.float32),
        name="lightning_forward",
        interpret=interpret,
    )(lengths, tables[2], query_pre, key_pre, value_pre, tables[0], tables[1])


def lightning_backward(lengths, query_pre, key_pre, value_pre, upstream, tables, interpret=False):
    length = query_pre.shape[0]
    return pl.pallas_call(
        backward_kernel,
        grid=(HEADS,),
        in_specs=scalar_specs() + head_specs(length, 4) + shared_specs(length),
        out_specs=head_specs(length, 3),
        out_shape=[jax.ShapeDtypeStruct((length, D), jnp.bfloat16)] * 3,
        scratch_shapes=[pltpu.VMEM((length // SPAN, 2 * HEAD, HEAD), jnp.bfloat16)],
        name="lightning_backward",
        interpret=interpret,
    )(lengths, tables[2], query_pre, key_pre, value_pre, upstream, tables[0], tables[1])


AXES = ("dp", "fsdp")
ROWS = 24


def lane_rows(matrix):
    extra = -matrix.shape[-1] % D
    if extra:
        matrix = jnp.pad(matrix, [(0, 0)] * (matrix.ndim - 1) + [(0, extra)])
    return jnp.split(matrix, matrix.shape[-1] // D, axis=-1)


def pick(parts, axis, index):
    return lax.dynamic_index_in_dim(parts, index, axis, keepdims=False)


def add_low(*pieces):
    total = pieces[0].astype(jnp.float32)
    for piece in pieces[1:]:
        total = total + piece.astype(jnp.float32)
    return total.astype(jnp.bfloat16)


class Bit:
    def __init__(self, name, stride):
        self.name, self.stride = name, stride
        self.place = lax.axis_index(name) // stride % 2

    def swap(self, value):
        members = lax.axis_size(self.name)
        pairs = [(source, source ^ self.stride) for source in range(members)]
        return lax.ppermute(value, self.name, pairs)

    def paired(self, own, other, axis):
        low = jnp.stack([own, other], axis=axis)
        high = jnp.stack([other, own], axis=axis)
        return jnp.where(self.place == 0, low, high)


class Cube:
    def __init__(self):
        rows = lax.axis_size("dp")
        columns = lax.axis_size("fsdp")
        short = 1 << ((columns.bit_length() - 1) // 2)
        strides = [("dp", 1 << digit) for digit in reversed(range(rows.bit_length() - 1))]
        strides += [("fsdp", 1 << digit) for digit in reversed(range(columns.bit_length() - 1))]
        self.bits = [Bit(name, stride) for name, stride in strides]
        labels = {key: index for index, key in enumerate(strides)}
        self.core = labels[("dp", 1)]
        across = [labels[key] for key in reversed(strides) if key[0] == "dp" and key[1] > 1]
        up = [labels[key] for key in reversed(strides) if key[0] == "fsdp" and key[1] < short]
        deep = [labels[("fsdp", short)]]
        self.far = [labels[key] for key in reversed(strides) if key[0] == "fsdp" and key[1] > short]
        self.streams = [across + up + deep, up + deep + across, deep + across + up]
        self.cuts = [0, 3 * D // 8, 6 * D // 8, D]

    def columns(self, value):
        return [value[..., low:high] for low, high in zip(self.cuts, self.cuts[1:])]


def packed(matrices):
    return jnp.concatenate(
        [piece for matrix in matrices for piece in lane_rows(jnp.transpose(matrix))], axis=0
    )


def unpacked(full, matrices, shards):
    gathered, start = [], 0
    for matrix in matrices:
        size, width = matrix.shape
        count = -(-size // D)
        columns = [
            full(start + index * width, start + (index + 1) * width).reshape(shards * width, D)
            for index in range(count)
        ]
        joined = columns[0] if count == 1 else jnp.concatenate(columns, axis=1)[:, :size]
        gathered.append(joined)
        start += count * width
    return gathered


class Gather:
    def __init__(self, matrices):
        self.matrices = matrices
        self.cube = Cube()
        self.value, self.known = packed(matrices), []
        self.done = 0

    def begin(self):
        for label in reversed(self.cube.far):
            self.value = self.join(self.value, label, self.known)
            self.known = sorted(self.known + [label])
        self.parts = self.cube.columns(self.value)

    def join(self, value, label, known):
        bit = self.cube.bits[label]
        axis = sum(other < label for other in known)
        return bit.paired(value, bit.swap(value), axis)

    def start(self):
        orders = [stream[::-1] for stream in self.cube.streams]
        self.moves = [(order[self.done], self.known + order[: self.done]) for order in orders]
        self.others = [
            self.cube.bits[label].swap(part) for part, (label, _) in zip(self.parts, self.moves)
        ]
        self.done += 1

    def settle(self):
        joined = []
        for own, other, (label, known) in zip(self.parts, self.others, self.moves):
            axis = sum(known_label < label for known_label in known)
            joined.append(self.cube.bits[label].paired(own, other, axis))
        self.parts = joined

    def advance(self, stages):
        for _ in range(stages):
            self.start()
            self.settle()

    def swap_cores(self):
        bit = self.cube.bits[self.cube.core]
        self.others = [bit.swap(part) for part in self.parts]

    def finish(self, shards):
        bit = self.cube.bits[self.cube.core]
        axis = self.cube.core
        halves = list(zip(self.parts, self.others))

        def rows(start, stop):
            pieces = [
                bit.paired(own[..., start:stop, :], other[..., start:stop, :], axis)
                for own, other in halves
            ]
            return jnp.concatenate(pieces, axis=-1)

        return unpacked(rows, self.matrices, shards)


class Scatter:
    def __init__(self, terms, single=False):
        self.cube = Cube()
        bit = self.cube.bits[self.cube.core]
        shape = (2,) * len(self.cube.bits)
        blocks = [term.reshape(shape + (-1, term.shape[-1])) for term in terms]
        self.own = [pick(block, self.cube.core, bit.place) for block in blocks]
        self.sent = [pick(block, self.cube.core, 1 - bit.place) for block in blocks]
        self.streams = self.cube.streams[:1] if single else self.cube.streams
        self.stage = 0

    def to_core(self):
        bit = self.cube.bits[self.cube.core]
        sums = [add_low(own, bit.swap(sent)) for own, sent in zip(self.own, self.sent)]
        value = jnp.stack(sums, axis=-3)
        self.parts = [value] if len(self.streams) == 1 else self.cube.columns(value)

    def halves(self, value, label, left):
        bit = self.cube.bits[label]
        axis = sum(other < label for other in left)
        return pick(value, axis, bit.place), pick(value, axis, 1 - bit.place)

    def send(self):
        self.own, self.sent, self.labels = [], [], []
        far = self.cube.far
        if self.stage == len(self.streams[0]):
            self.parts = [jnp.concatenate(self.parts, axis=-1)]
        for index, part in enumerate(self.parts):
            order = self.streams[index] + far
            left = order[self.stage :] if self.stage >= len(self.streams[0]) else (
                far + self.streams[index][self.stage :]
            )
            own, sent = self.halves(part, order[self.stage], left)
            self.own.append(own)
            self.sent.append(sent)
            self.labels.append(order[self.stage])
        self.stage += 1

    def meet(self):
        bits = self.cube.bits
        self.parts = [
            add_low(own, bits[label].swap(sent))
            for own, sent, label in zip(self.own, self.sent, self.labels)
        ]

    def finish(self):
        while self.stage < len(self.streams[0]) + len(self.cube.far):
            self.send()
            self.meet()
        (value,) = self.parts
        return [jnp.transpose(value[index].astype(jnp.float32)) for index in range(value.shape[0])]


def scatter_call(terms, shards):
    pieces, widths = [], []
    for term in terms:
        size = term.shape[1]
        block = term.reshape(shards, -1, size)
        widths.append((size, block.shape[1]))
        pieces += lane_rows(block)
    rows = sum(piece.shape[1] for piece in pieces)
    if rows % ROWS:
        pieces.append(jnp.zeros((shards, -rows % ROWS, D), pieces[0].dtype))
    return jnp.concatenate(pieces, axis=1).reshape(-1, D), widths


def scatter_sums(stacked, widths):
    summed = lax.psum_scatter(stacked, AXES, scatter_dimension=0, tiled=True)
    summed = summed.astype(jnp.float32)
    outs, start = [], 0
    for size, width in widths:
        count = -(-size // D)
        columns = [
            summed[start + index * width : start + (index + 1) * width] for index in range(count)
        ]
        joined = columns[0] if count == 1 else jnp.concatenate(columns, axis=1)[:, :size]
        outs.append(jnp.transpose(joined))
        start += count * width
    return outs


def tie(values):
    return lax.optimization_barrier(values)


def after(earlier, value):
    return tie((earlier, value))[1]


def weight_term(left, right):
    return weight_dot(left, right).astype(jnp.bfloat16)


def per_device(
    inputs,
    lengths,
    query_weight,
    key_weight,
    value_weight,
    gate_weight,
    out_weight,
    first_weight,
    second_weight,
    down_weight,
    cotangent,
):
    shards = lax.axis_size(AXES)
    heads = Gather((query_weight, key_weight, value_weight, gate_weight, out_weight))
    glu = Gather((first_weight, second_weight, down_weight))
    last = len(glu.cube.streams[0])
    heads.begin()
    glu.value = after(heads.parts, glu.value)
    heads.advance(last - 1)
    glu.begin()
    glu.parts = after(heads.parts, glu.parts)
    heads.advance(1)
    glu.advance(last - 2)
    glu.parts = after(heads.parts, glu.parts)
    heads.swap_cores()
    query_t, key_t, value_t, gate_t, out_t = heads.finish(shards)
    glu.start()
    inputs_f = inputs.astype(jnp.float32)
    length = inputs.shape[0]
    mask = (lax.iota(jnp.int32, length) < lengths[0]).astype(jnp.float32)[:, None]
    tables = make_tables(length)
    normed = simple_norm(inputs_f).astype(jnp.bfloat16)
    query_pre = back_dot(normed, query_t)
    key_pre = back_dot(normed, key_t)
    value_pre = back_dot(normed, value_t)
    gate_pre = back_dot(normed, gate_t)
    glu.others = after((query_pre, key_pre, value_pre), glu.others)
    glu.settle()
    glu.start()
    attended = lightning_forward(lengths, query_pre, key_pre, value_pre, tables)
    glu.others = after(attended, glu.others)
    glu.settle()
    glu.swap_cores()
    attended_norm = simple_norm(attended)
    gated = (attended_norm * gate_pre * mask).astype(jnp.bfloat16)
    mixed = inputs_f + back_dot(gated, out_t)
    normed_two = simple_norm(mixed).astype(jnp.bfloat16)
    glu.others = after(normed_two, glu.others)
    first_t, second_t, down_t = glu.finish(shards)
    first = back_dot(normed_two, first_t).astype(jnp.bfloat16)
    second = back_dot(normed_two, second_t).astype(jnp.bfloat16)
    product_low = (first.astype(jnp.float32) * second * mask).astype(jnp.bfloat16)
    down = Scatter([weight_term(cotangent, product_low)], single=True)
    product_grad = forward_dot(after(down.sent, cotangent), down_t)
    first_low = (product_grad * second * mask).astype(jnp.bfloat16)
    second_low = (product_grad * first * mask).astype(jnp.bfloat16)
    down.to_core()
    down.send()
    first_low, second_low, down.sent = tie((first_low, second_low, down.sent))
    stacked, widths = scatter_call(
        [weight_term(first_low, normed_two), weight_term(second_low, normed_two)], shards
    )
    first_low, second_low, product_low, stacked = tie(
        (first_low, second_low, product_low, stacked)
    )
    first_sum, second_sum = scatter_sums(stacked, widths)
    normed_two_grad = forward_dot(first_low, first_t) + forward_dot(second_low, second_t)
    down.meet()
    down.send()
    normed_two_grad, down.sent = tie((normed_two_grad, down.sent))
    mixed_grad = cotangent.astype(jnp.float32) + norm_back(mixed, normed_two_grad)
    mixed_low = mixed_grad.astype(jnp.bfloat16)
    gated_grad = forward_dot(mixed_low, out_t)
    gate_low = (gated_grad * attended_norm * mask).astype(jnp.bfloat16)
    attended_low = norm_back(attended, gated_grad * gate_pre * mask).astype(jnp.bfloat16)
    down.meet()
    down.send()
    attended_low, down.sent = tie((attended_low, down.sent))
    query_low, key_low, value_low = lightning_backward(
        lengths, query_pre, key_pre, value_pre, attended_low, tables
    )
    attention = Scatter(
        [
            weight_term(mixed_low, gated),
            weight_term(gate_low, normed),
            weight_term(query_low, normed),
            weight_term(key_low, normed),
            weight_term(value_low, normed),
        ]
    )
    down.meet()
    attention.to_core()
    attention.send()
    query_low, key_low, value_low, gate_low, product_low, attention.sent, down.parts = tie(
        (query_low, key_low, value_low, gate_low, product_low, attention.sent, down.parts)
    )
    result = mixed + back_dot(product_low, down_t)
    normed_grad = (
        forward_dot(query_low, query_t)
        + forward_dot(key_low, key_t)
        + forward_dot(value_low, value_t)
        + forward_dot(gate_low, gate_t)
    )
    input_grad = mixed_grad + norm_back(inputs_f, normed_grad)
    attention.meet()
    (down_sum,) = down.finish()
    out_sum, gate_sum, query_sum, key_sum, value_sum = attention.finish()
    return (
        result.astype(jnp.bfloat16),
        input_grad,
        query_sum,
        key_sum,
        value_sum,
        gate_sum,
        out_sum,
        first_sum,
        second_sum,
        down_sum,
    )


def solution(mesh):
    return jax.shard_map(
        per_device,
        mesh=mesh,
        in_specs=(
            P(("dp", "fsdp"), None),
            P(("dp", "fsdp")),
            P(None, ("dp", "fsdp")),
            P(None, ("dp", "fsdp")),
            P(None, ("dp", "fsdp")),
            P(None, ("dp", "fsdp")),
            P(None, ("dp", "fsdp")),
            P(None, ("dp", "fsdp")),
            P(None, ("dp", "fsdp")),
            P(None, ("dp", "fsdp")),
            P(("dp", "fsdp"), None),
        ),
        out_specs=(
            P(("dp", "fsdp"), None),
            P(("dp", "fsdp"), None),
            P(None, ("dp", "fsdp")),
            P(None, ("dp", "fsdp")),
            P(None, ("dp", "fsdp")),
            P(None, ("dp", "fsdp")),
            P(None, ("dp", "fsdp")),
            P(None, ("dp", "fsdp")),
            P(None, ("dp", "fsdp")),
            P(None, ("dp", "fsdp")),
        ),
        check_vma=False,
    )
```
